512 devices in a mesh: req: 64 (over y_hi, z, core), tp: 8 (over y_lo, x).
Axes of the slice: x: 4, y: 4 (y_hi: 2, y_lo: 2; y = y_hi * 2 + y_lo), z: 16, core: 2. Of those that a mesh axis runs over, the one named last changes fastest.
Arguments:
- queries: bfloat16 [16384, 5120], P('req', 'tp')
- new_keys: bfloat16 [16384, 5120], P('req', 'tp')
- new_values: bfloat16 [16384, 5120], P('req', 'tp'), may hold values from -6 to 6
- query_gain: float32 [5120], P('tp'), may hold values from 0.1 to 1.9
- key_gain: float32 [5120], P('tp'), may hold values from 0.4 to 2.5
- cache_keys: bfloat16 [7168, 8, 5120], P('req', None, 'tp')
- cache_values: bfloat16 [7168, 8, 5120], P('req', None, 'tp'), may hold values from -6 to 6
- page_table: int32 [64, 48], P('req'), may hold values from 0 to 111, as said below
- cache_lens: int32 [64], P('req'), may hold values from 48 to 384, as said below
- mig_pages: int32 [64, 64], P('req'), may hold values from 0 to 111, as said below
- mig_dest: int32 [4096, 1], P('req'), may hold values from 0 to 63; in each aligned block of 64 rows (0 to 63, 64 to 127, ...) at most 2 rows name the same one
- cross_queries: bfloat16 [16384, 5120], P('req', 'tp')
- text_keys: bfloat16 [8192, 5120], P('req', 'tp')
- text_values: bfloat16 [8192, 5120], P('req', 'tp'), may hold values from -6 to 6
- out_weight: bfloat16 [5120, 5120], P('tp', 'req'), may hold values from -1 to 1
- residual: bfloat16 [16384, 5120], P('req', 'tp')
- gate: bfloat16 [64, 5120], P('req', 'tp'), may hold values from -6 to 6
- shift: bfloat16 [64, 5120], P('req', 'tp'), may hold values from -3 to 3
- scale: bfloat16 [64, 5120], P('req', 'tp'), may hold values from -3 to 3
Outputs:
- stream: bfloat16 [16384, 5120], P('req', 'tp')
- normed: bfloat16 [16384, 5120], P('req', 'tp')
- cross_out: bfloat16 [16384, 5120], P('req', 'tp')
The draws below stay inside these ranges and needn't reach their ends.
Inputs may be any that keep to these rules, and one draw needn't show every extreme that they name: Row r of page_table and row r of mig_pages together name every one of the 112 pages of row r's pool exactly once. `mig_pages`: see page_table. `cache_lens`: at least 48; the largest is exactly 384. `mig_dest`: among the 64 pages of one request row (the rows of one device) no destination is named more than 2 times.
All inputs are finite; a program needn't handle non-finite values.
Results may differ from the reference program's by a relative error of at most 0.014.
Values may be sent and summed in bfloat16 or wider, within the bound.
A program may use at most 64 MiB of HBM per device.

```python
import math
import jax
import jax.numpy as jnp
import numpy as np
from jax import lax

HEADS = 40
HD = 128
D = 5120
TOK_DEV = 256
TEXT = 128
MAXP = 48
PAGE = 8
CAP = 2
MIG = 64
POOL = 112
TOKENS = 16384
N_REQ = 64
N_TP = 8


def scaled_field(key, row_count, row_low, row_high, column_low, column_high):
    base = jax.random.normal(jax.random.fold_in(key, 1), (row_count, D), jnp.float32)
    row_scale = jnp.exp(jax.random.uniform(jax.random.fold_in(key, 2), (row_count, 1), jnp.float32, math.log(row_low), math.log(row_high)))
    column_scale = jnp.exp(jax.random.uniform(jax.random.fold_in(key, 3), (1, D), jnp.float32, math.log(column_low), math.log(column_high)))
    ramp = 1.0 + 2.0 * jnp.arange(D, dtype=jnp.float32)[None, :] / (D - 1)
    return base * row_scale * column_scale * ramp


def pool_order(key):
    row_keys = jax.random.split(jax.random.fold_in(key, 11), N_REQ)
    return jax.vmap(lambda row_key: jax.random.permutation(row_key, POOL))(row_keys).astype(jnp.int32)


def draw_queries(key, part):
    field = scaled_field(jax.random.fold_in(key, 40), TOKENS, 1.0, 10.0, 1.0, 10.0)
    return field.astype(jnp.bfloat16)


def draw_new_keys(key, part):
    field = scaled_field(jax.random.fold_in(key, 50), TOKENS, 1.0, 10.0, 1.0, 10.0)
    return field.astype(jnp.bfloat16)


def draw_cache_keys(key, part):
    field = 2.5 * jax.random.normal(jax.random.fold_in(key, 60), (N_REQ * POOL, PAGE, D), jnp.float32)
    return field.astype(jnp.bfloat16)


def draw_page_table(key, part):
    return pool_order(key)[:, :MAXP]


def draw_mig_pages(key, part):
    return pool_order(key)[:, MAXP:]


def draw_cache_lens(key, part):
    lens_key = jax.random.fold_in(key, 21)
    lengths = jax.random.randint(jax.random.fold_in(lens_key, 1), (N_REQ,), MAXP * PAGE // 8, MAXP * PAGE + 1)
    longest = jax.random.randint(jax.random.fold_in(lens_key, 2), (), 0, N_REQ)
    return jnp.where(jnp.arange(N_REQ) == longest, MAXP * PAGE, lengths).astype(jnp.int32)


def draw_cross_queries(key, part):
    field = jax.random.normal(jax.random.fold_in(key, 70), (TOKENS, D), jnp.float32)
    return field.astype(jnp.bfloat16)


def draw_text_keys(key, part):
    field = 2.5 * jax.random.normal(jax.random.fold_in(key, 80), (N_REQ * TEXT, D), jnp.float32)
    return field.astype(jnp.bfloat16)


def draw_residual(key, part):
    field = scaled_field(jax.random.fold_in(key, 90), TOKENS, 0.1, 1.0, 0.3, 3.0)
    return field.astype(jnp.bfloat16)


def raised(array, stream_key, source, target, parts, factor):
    owner, partner = [(jnp.arange(array.shape[dim]) // (array.shape[dim] // parts)).reshape([-1 if axis == dim else 1 for axis in range(array.ndim)]) for dim in (source, target)]
    chosen = jax.random.permutation(stream_key, parts)[partner]
    strong = (owner == chosen) | (owner == (partner + parts // 2) % parts)
    return jnp.where(strong, factor * array, array)


def shard_levels(stream_key, dims, cuts, smallest, high):
    factor_of, own = 1.0, jax.random.fold_in(stream_key, 6)
    for dim, parts in cuts:
        heights = jnp.exp(jax.random.uniform(jax.random.fold_in(own, dim), (parts,), jnp.float32, smallest / len(cuts), high / len(cuts)))
        factor_of = factor_of * jnp.repeat(heights, dims[dim] // parts).reshape([-1 if axis == dim else 1 for axis in range(len(dims))])
    return factor_of


def deal_out(stream_key, own, number, rows, count, top, bound, skew):
    sequence = jax.random.permutation(stream_key, count)
    heavy_load, ordinary = load_shares(count, rows * top, bound, skew, True), load_shares(count, rows * top, bound, skew, False)
    places = jnp.arange(count)

    def named(tallies, offset_by):
        used = int((tallies > 0).sum())
        fixed = max(1, used // 4)
        moved = fixed + (places - fixed + offset_by * (used - fixed)) % max(1, count - fixed)
        return jnp.zeros((count,), jnp.int32).at[sequence[jnp.where(places < fixed, places, moved)]].set(jnp.asarray(tallies, jnp.int32))

    tallies = jnp.where(number % 4 == 0, named(heavy_load, number // 4), named(ordinary, number - number // 4 - 1))
    mixed = jax.random.permutation(jax.random.fold_in(own, 3), count)
    giver, taker = mixed[0:count // 2 * 2:2], mixed[1:count // 2 * 2:2]
    slack = jnp.minimum(tallies[giver] - 1, bound - tallies[taker]) // 2
    slack = jnp.where((giver == sequence[0]) | (taker == sequence[0]) | (tallies[taker] == 0), 0, jnp.maximum(slack, 0))
    moved = jax.random.randint(jax.random.fold_in(own, 4), (count // 2,), 0, 1 << 20) % (slack + 1)
    tallies = tallies.at[giver].add(-moved).at[taker].add(moved)
    labels = jnp.searchsorted(jnp.cumsum(tallies), jnp.arange(rows * top), side="right").astype(jnp.int32)
    table = labels.reshape(top, rows).T
    table = table[jax.random.permutation(jax.random.fold_in(own, 1), rows)]
    offset_by = jax.random.randint(jax.random.fold_in(own, 2), (rows, 1), 0, top)
    return jnp.take_along_axis(table, (jnp.arange(top)[None, :] + offset_by) % top, axis=1)


def load_shares(number_of, total, reach, slope, full):
    portions = [(1 << 20) // math.isqrt(rank ** slope) + 1 for rank in range(1, number_of + 1)]
    largest = reach if full else min(reach, max(-(-total // number_of), total * portions[0] // sum(portions)))
    least = 1 if total - largest >= number_of - 1 else 0
    holding, surplus = [largest] + [least] * (number_of - 1), total - largest - least * (number_of - 1)
    while surplus > 0:
        movable = [i for i in range(1, number_of) if holding[i] < largest] or [i for i in range(1, number_of) if holding[i] < reach]
        pool, budget = sum([portions[i] for i in movable]), surplus
        for i in movable:
            extra = min(reach - holding[i], max(1, budget * portions[i] // pool), surplus)
            holding[i] = holding[i] + extra
            surplus = surplus - extra
    return np.array(holding)


def bell_draw(rng, shape, width, reach, cuts=(), held_as=jnp.bfloat16):
    result = width * jax.random.normal(rng, shape, jnp.float32)
    if cuts:
        result = result * shard_levels(rng, shape, cuts, -0.22, 0.18)
    return jnp.clip(result, -reach, reach).astype(held_as)


def bell_draw_with(stream_key, dims, spread, limit, pieces, heavy, kind=jnp.bfloat16):
    result = spread * jax.random.normal(stream_key, dims, jnp.float32)
    if pieces:
        result = result * shard_levels(stream_key, dims, pieces, -0.22, 0.18)
    return jnp.clip(raised(result, jax.random.fold_in(stream_key, 3), *heavy), -limit, limit).astype(kind)


def setup_inputs(seed: int = 0) -> dict:
    key_of = jax.random.split(jax.random.key(seed), 20)
    queries = draw_queries(jax.random.fold_in(key_of[19], 71), 0)
    new_keys = draw_new_keys(jax.random.fold_in(key_of[19], 71), 0)
    new_values = bell_draw(key_of[2], (TOKENS, D), 1.0, 6.0, ((0, 64), (1, 8)))
    query_gain = jnp.clip(1.0 + 0.18 * jax.random.normal(key_of[3], (D,), jnp.float32), 0.1, 1.9)
    key_gain = jnp.clip(jnp.exp(math.log(2.5) - 1.8325814 * jax.random.uniform(key_of[4], (D,), jnp.float32) ** shard_levels(key_of[4], (D,), ((0, 8),), -0.2, 0.2)), 0.4, 2.5)
    cache_keys = draw_cache_keys(jax.random.fold_in(key_of[19], 71), 0)
    cache_values = bell_draw(key_of[6], (N_REQ * POOL, PAGE, D), 1.0, 6.0, ((0, 64), (2, 8)))
    page_table = draw_page_table(jax.random.fold_in(key_of[19], 71), 0)
    cache_lens = draw_cache_lens(jax.random.fold_in(key_of[19], 71), 0)
    mig_pages = draw_mig_pages(jax.random.fold_in(key_of[19], 71), 0)
    mig_dest_keys = jax.random.split(jax.random.fold_in(key_of[10], 1), (N_REQ * MIG) // MIG)
    mig_dest_turns = jax.random.permutation(jax.random.fold_in(key_of[10], 3), (N_REQ * MIG) // MIG)
    mig_dest = jax.vmap(lambda own, number: deal_out(jax.random.fold_in(key_of[10], 2), own, number, MIG, N_REQ, 1, CAP, 2))(mig_dest_keys, mig_dest_turns).reshape((N_REQ * MIG, 1))
    cross_queries = draw_cross_queries(jax.random.fold_in(key_of[19], 71), 0)
    text_keys = draw_text_keys(jax.random.fold_in(key_of[19], 71), 0)
    text_values = bell_draw(key_of[13], (N_REQ * TEXT, D), 1.0, 6.0, ((0, 64), (1, 8)))
    out_weight = bell_draw_with(key_of[14], (D, D), (D // 16) ** -0.5, 1.0, ((0, 8), (1, 64)), (0, 1, 64, 4.0))
    residual = draw_residual(jax.random.fold_in(key_of[19], 71), 0)
    gate = bell_draw(key_of[16], (N_REQ, D), 1.5, 6.0, ((0, 64), (1, 8)))
    shift = bell_draw(key_of[17], (N_REQ, D), 0.5, 3.0, ((0, 64), (1, 8)))
    scale = bell_draw(key_of[18], (N_REQ, D), 0.5, 3.0, ((0, 64), (1, 8)))
    return {"queries": queries, "new_keys": new_keys, "new_values": new_values, "query_gain": query_gain, "key_gain": key_gain, "cache_keys": cache_keys, "cache_values": cache_values, "page_table": page_table, "cache_lens": cache_lens, "mig_pages": mig_pages, "mig_dest": mig_dest, "cross_queries": cross_queries, "text_keys": text_keys, "text_values": text_values, "out_weight": out_weight, "residual": residual, "gate": gate, "shift": shift, "scale": scale}


EPS = 1e-06

def rms_normed(values, gain):
    floats = values.astype(jnp.float32)
    mean_square = lax.optimization_barrier(jnp.mean(floats * floats, axis=1, keepdims=True))
    return (floats * lax.rsqrt(mean_square + EPS) * gain).astype(jnp.bfloat16)

def attend(query_rows, key_rows, value_rows, usable):
    row_count = query_rows.shape[0]
    query_heads = query_rows.astype(jnp.float32).reshape(row_count, HEADS, HD)
    key_heads = key_rows.astype(jnp.float32).reshape(key_rows.shape[0], HEADS, HD)
    value_heads = value_rows.astype(jnp.float32).reshape(value_rows.shape[0], HEADS, HD)
    scores = jnp.einsum('qhd,khd->hqk', query_heads, key_heads) * (1.0 / math.sqrt(HD))
    if usable is not None:
        scores = jnp.where(usable[None, None, :], scores, -jnp.inf)
    row_max = lax.optimization_barrier(jnp.max(scores, axis=2, keepdims=True))
    exponent = jnp.exp(scores - row_max)
    denominator = lax.optimization_barrier(jnp.sum(exponent, axis=2))
    weights = lax.optimization_barrier(exponent.astype(jnp.bfloat16)).astype(jnp.float32)
    mixed = jnp.einsum('hqk,khd->qhd', weights, value_heads)
    mixed = mixed / jnp.transpose(denominator)[:, :, None]
    return mixed.reshape(row_count, HEADS * HD).astype(jnp.bfloat16)

def reference(queries, new_keys, new_values, query_gain, key_gain, cache_keys, cache_values, page_table, cache_lens, mig_pages, mig_dest, cross_queries, text_keys, text_values, out_weight, residual, gate, shift, scale):
    query_normed = rms_normed(queries, query_gain)
    key_normed = rms_normed(new_keys, key_gain)
    destination = mig_dest[:, 0].reshape(N_REQ, MIG)
    slot_match = (destination[:, :, None] == jnp.arange(N_REQ, dtype=jnp.int32)[None, None, :]).astype(jnp.int32)
    position = lax.optimization_barrier(jnp.sum(jnp.cumsum(slot_match, axis=1) * slot_match, axis=2)) - 1
    sources = jnp.broadcast_to(jnp.arange(N_REQ, dtype=jnp.int32)[:, None], (N_REQ, MIG))
    global_page = sources * POOL + mig_pages
    arrivals = jnp.full((N_REQ, N_REQ, CAP), -1, jnp.int32).at[destination, sources, position].set(global_page)

    def one_request(request):
        first = request * TOK_DEV
        query_rows = lax.dynamic_slice_in_dim(query_normed, first, TOK_DEV, 0)
        own_keys = lax.dynamic_slice_in_dim(key_normed, first, TOK_DEV, 0)
        own_values = lax.dynamic_slice_in_dim(new_values, first, TOK_DEV, 0)
        own_pages = request * POOL + page_table[request]
        resident_keys = cache_keys[own_pages].reshape(MAXP * PAGE, D)
        resident_values = cache_values[own_pages].reshape(MAXP * PAGE, D)
        resident_usable = jnp.arange(MAXP * PAGE, dtype=jnp.int32) < cache_lens[request]
        incoming = arrivals[request].reshape(-1)
        incoming_usable = jnp.repeat(incoming >= 0, PAGE)
        safe_pages = jnp.maximum(incoming, 0)
        arrived_keys = cache_keys[safe_pages].reshape(-1, D)
        arrived_values = cache_values[safe_pages].reshape(-1, D)
        all_keys = jnp.concatenate([resident_keys, arrived_keys, own_keys], axis=0)
        all_values = jnp.concatenate([resident_values, arrived_values, own_values], axis=0)
        usable = jnp.concatenate([resident_usable, incoming_usable, jnp.ones((TOK_DEV,), bool)])
        attended = attend(query_rows, all_keys, all_values, usable)
        cross_rows = lax.dynamic_slice_in_dim(cross_queries, first, TOK_DEV, 0)
        text_rows = lax.dynamic_slice_in_dim(text_keys, request * TEXT, TEXT, 0)
        text_vals = lax.dynamic_slice_in_dim(text_values, request * TEXT, TEXT, 0)
        crossed = attend(cross_rows, text_rows, text_vals, None)
        return (attended, crossed)
    attended, crossed = lax.map(one_request, jnp.arange(N_REQ, dtype=jnp.int32))
    attended = attended.reshape(TOKENS, D)
    cross_out = crossed.reshape(TOKENS, D)
    group_width = D // N_TP
    projected = jnp.zeros((TOKENS, D), jnp.float32)
    for group in range(N_TP):
        lower = group * group_width
        partial_term = jnp.dot(attended[:, lower:lower + group_width], out_weight[lower:lower + group_width, :], preferred_element_type=jnp.float32)
        projected = projected + lax.optimization_barrier(partial_term.astype(jnp.bfloat16)).astype(jnp.float32)
    gate_rows = jnp.repeat(gate.astype(jnp.float32), TOK_DEV, axis=0)
    shift_rows = jnp.repeat(shift.astype(jnp.float32), TOK_DEV, axis=0)
    scale_rows = jnp.repeat(scale.astype(jnp.float32), TOK_DEV, axis=0)
    updated = residual.astype(jnp.float32) + gate_rows * projected
    stream = updated.astype(jnp.bfloat16)
    row_mean = lax.optimization_barrier(jnp.mean(updated, axis=1, keepdims=True))
    row_var = lax.optimization_barrier(jnp.mean(jnp.square(updated - row_mean), axis=1, keepdims=True))
    normed = ((updated - row_mean) * lax.rsqrt(row_var + EPS) * (1.0 + scale_rows) + shift_rows).astype(jnp.bfloat16)
    return (stream, normed, cross_out)
```

```python
import math

import jax
import jax.numpy as jnp
from jax import lax
from jax.experimental import pallas as pl
from jax.experimental.pallas import tpu as pltpu
from jax.sharding import PartitionSpec as P

HD = 128
CAP = 2


EPS = 1e-06


def head_scores(query, keys, scale):
    return (
        lax.dot_general(query, keys, (((1,), (1,)), ((), ())), preferred_element_type=jnp.float32)
        * scale
    )


def self_kernel(q_ref, kr_ref, vr_ref, ka_ref, va_ref, kn_ref, vn_ref, ur_ref, ua_ref, o_ref):
    scale = 1.0 / math.sqrt(HD)
    query = q_ref[...]
    resident = jnp.where(ur_ref[...] > 0, head_scores(query, kr_ref[...], scale), -jnp.inf)
    arrived = jnp.where(ua_ref[...] > 0, head_scores(query, ka_ref[...], scale), -jnp.inf)
    own = head_scores(query, kn_ref[...], scale)
    row_max = jnp.maximum(
        jnp.max(own, axis=1, keepdims=True),
        jnp.maximum(
            jnp.max(resident, axis=1, keepdims=True), jnp.max(arrived, axis=1, keepdims=True)
        ),
    )
    denominator = jnp.zeros_like(row_max)
    mixed = jnp.zeros(o_ref.shape, jnp.float32)
    for scores, values in ((resident, vr_ref), (arrived, va_ref), (own, vn_ref)):
        exponent = jnp.exp(scores - row_max)
        denominator += jnp.sum(exponent, axis=1, keepdims=True)
        mixed += jnp.dot(
            exponent.astype(jnp.bfloat16), values[...], preferred_element_type=jnp.float32
        )
    o_ref[...] = (mixed / denominator).astype(jnp.bfloat16)


def cross_kernel(q_ref, k_ref, v_ref, o_ref):
    scores = head_scores(q_ref[...], k_ref[...], 1.0 / math.sqrt(HD))
    exponent = jnp.exp(scores - jnp.max(scores, axis=1, keepdims=True))
    denominator = jnp.sum(exponent, axis=1, keepdims=True)
    mixed = jnp.dot(exponent.astype(jnp.bfloat16), v_ref[...], preferred_element_type=jnp.float32)
    o_ref[...] = (mixed / denominator).astype(jnp.bfloat16)


def per_head(kernel, rows, masks, width):
    spec = lambda array: pl.BlockSpec((array.shape[0], HD), lambda h: (0, h))
    flag = lambda array: pl.BlockSpec(array.shape, lambda h: (0, 0))
    keys = sum(array.shape[0] for array in rows[1:]) // 2
    tokens = rows[0].shape[0]
    return pl.pallas_call(
        kernel,
        grid=(width // HD,),
        out_shape=jax.ShapeDtypeStruct((tokens, width), jnp.bfloat16),
        in_specs=[spec(array) for array in rows] + [flag(array) for array in masks],
        out_specs=pl.BlockSpec((tokens, HD), lambda h: (0, h)),
        cost_estimate=pl.CostEstimate(
            flops=4 * tokens * keys * width,
            bytes_accessed=4 * (tokens + keys) * width,
            transcendentals=tokens * keys * width // HD,
        ),
    )(*rows, *masks)


def shards(
    queries,
    new_keys,
    new_values,
    query_gain,
    key_gain,
    cache_keys,
    cache_values,
    page_table,
    cache_lens,
    mig_pages,
    mig_dest,
    cross_queries,
    text_keys,
    text_values,
    out_weight,
    residual,
    gate,
    shift,
    scale,
):
    token_count, local_width = queries.shape
    tp_count = lax.axis_size("tp")
    full_width = local_width * tp_count
    peer_count = lax.axis_size("req")
    page_len = cache_keys.shape[1]
    peers = jnp.arange(peer_count, dtype=jnp.int32)

    destination = mig_dest[:, 0]
    slot_match = (destination[:, None] == peers[None, :]).astype(jnp.int32)
    position = jnp.sum(jnp.cumsum(slot_match, axis=0) * slot_match, axis=1) - 1
    target_slot = destination * CAP + position
    selection = jnp.arange(peer_count * CAP, dtype=jnp.int32)[:, None] == target_slot[None, :]
    slot_page = jnp.sum(jnp.where(selection, mig_pages, 0), axis=1)
    sent_keys = cache_keys[slot_page]
    sent_values = cache_values[slot_page]
    arrived_keys = lax.all_to_all(sent_keys, "req", split_axis=0, concat_axis=0, tiled=True)
    arrived_values = lax.all_to_all(sent_values, "req", split_axis=0, concat_axis=0, tiled=True)

    all_dest = lax.all_gather(mig_dest, "req", axis=1, tiled=True)
    arrivals = jnp.sum((all_dest == lax.axis_index("req")).astype(jnp.int32), axis=0)
    filled = arrivals[:, None] > jnp.arange(CAP, dtype=jnp.int32)[None, :]
    arrived_usable = jnp.broadcast_to(
        filled[:, :, None].astype(jnp.float32), (peer_count, CAP, page_len)
    ).reshape(1, -1)

    query_float = queries.astype(jnp.float32)
    key_float = new_keys.astype(jnp.float32)
    query_squares, key_squares = lax.psum(
        (jnp.sum(query_float * query_float, axis=1), jnp.sum(key_float * key_float, axis=1)), "tp"
    )
    query_normed = (
        query_float * lax.rsqrt(query_squares / full_width + EPS)[:, None] * query_gain
    ).astype(jnp.bfloat16)
    key_normed = (key_float * lax.rsqrt(key_squares / full_width + EPS)[:, None] * key_gain).astype(
        jnp.bfloat16
    )
    own_pages = page_table[0]
    resident_keys = cache_keys[own_pages].reshape(-1, local_width)
    resident_values = cache_values[own_pages].reshape(-1, local_width)
    resident_usable = (
        jnp.arange(resident_keys.shape[0], dtype=jnp.int32) < cache_lens[0]
    ).astype(jnp.float32)[None, :]

    cross_out = per_head(cross_kernel, (cross_queries, text_keys, text_values), (), local_width)
    attended = per_head(
        self_kernel,
        (
            query_normed,
            resident_keys,
            resident_values,
            arrived_keys.reshape(-1, local_width),
            arrived_values.reshape(-1, local_width),
            key_normed,
            new_values,
        ),
        (resident_usable, arrived_usable),
        local_width,
    )
    whole_weight = lax.all_gather(out_weight, "req", axis=1, tiled=True)
    partial_rows = jnp.dot(attended, whole_weight, preferred_element_type=jnp.float32).astype(
        jnp.bfloat16
    )
    pieces = lax.all_to_all(
        jnp.stack(jnp.split(partial_rows, tp_count, axis=1)),
        "tp",
        split_axis=0,
        concat_axis=0,
        tiled=True,
    )
    projected = jnp.sum(pieces.astype(jnp.float32), axis=0)
    updated = residual.astype(jnp.float32) + gate.astype(jnp.float32) * projected
    local_mean = jnp.mean(updated, axis=1)
    local_var = jnp.mean(jnp.square(updated - local_mean[:, None]), axis=1)
    means, variances = lax.all_gather(jnp.stack([local_mean, local_var]), "tp", axis=1)
    row_mean = jnp.mean(means, axis=0)
    row_var = jnp.mean(variances + jnp.square(means - row_mean[None, :]), axis=0)
    stream = updated.astype(jnp.bfloat16)
    normed = (
        (updated - row_mean[:, None])
        * lax.rsqrt(row_var + EPS)[:, None]
        * (1.0 + scale.astype(jnp.float32))
        + shift.astype(jnp.float32)
    ).astype(jnp.bfloat16)
    return (stream, normed, cross_out)


def solution(mesh):
    in_specs = (
        P("req", "tp"),
        P("req", "tp"),
        P("req", "tp"),
        P("tp"),
        P("tp"),
        P("req", None, "tp"),
        P("req", None, "tp"),
        P("req", None),
        P("req"),
        P("req", None),
        P("req", None),
        P("req", "tp"),
        P("req", "tp"),
        P("req", "tp"),
        P("tp", "req"),
        P("req", "tp"),
        P("req", "tp"),
        P("req", "tp"),
        P("req", "tp"),
    )
    out_specs = (P("req", "tp"), P("req", "tp"), P("req", "tp"))
    return jax.shard_map(shards, mesh=mesh, in_specs=in_specs, out_specs=out_specs, check_vma=False)
```

```python
import functools
import math

import jax
import jax.numpy as jnp
from jax import lax
from jax.experimental import pallas as pl
from jax.experimental.pallas import tpu as pltpu
from jax.sharding import PartitionSpec as P

HD = 128
CAP = 2


EPS = 1e-06


def head_scores(query, keys, scale):
    return (
        lax.dot_general(query, keys, (((1,), (1,)), ((), ())), preferred_element_type=jnp.float32)
        * scale
    )


def self_kernel(q_ref, kr_ref, vr_ref, ka_ref, va_ref, kn_ref, vn_ref, ur_ref, ua_ref, o_ref):
    scale = 1.0 / math.sqrt(HD)
    query = q_ref[...]
    resident = jnp.where(ur_ref[...] > 0, head_scores(query, kr_ref[...], scale), -jnp.inf)
    arrived = jnp.where(ua_ref[...] > 0, head_scores(query, ka_ref[...], scale), -jnp.inf)
    own = head_scores(query, kn_ref[...], scale)
    row_max = jnp.maximum(
        jnp.max(own, axis=1, keepdims=True),
        jnp.maximum(
            jnp.max(resident, axis=1, keepdims=True), jnp.max(arrived, axis=1, keepdims=True)
        ),
    )
    denominator = jnp.zeros_like(row_max)
    mixed = jnp.zeros(o_ref.shape, jnp.float32)
    for scores, values in ((resident, vr_ref), (arrived, va_ref), (own, vn_ref)):
        exponent = jnp.exp(scores - row_max)
        denominator += jnp.sum(exponent, axis=1, keepdims=True)
        mixed += jnp.dot(
            exponent.astype(jnp.bfloat16), values[...], preferred_element_type=jnp.float32
        )
    o_ref[...] = (mixed / denominator).astype(jnp.bfloat16)


def cross_kernel(q_ref, k_ref, v_ref, o_ref):
    scores = head_scores(q_ref[...], k_ref[...], 1.0 / math.sqrt(HD))
    exponent = jnp.exp(scores - jnp.max(scores, axis=1, keepdims=True))
    denominator = jnp.sum(exponent, axis=1, keepdims=True)
    mixed = jnp.dot(exponent.astype(jnp.bfloat16), v_ref[...], preferred_element_type=jnp.float32)
    o_ref[...] = (mixed / denominator).astype(jnp.bfloat16)


def per_head(kernel, rows, masks, width):
    spec = lambda array: pl.BlockSpec((array.shape[0], HD), lambda h: (0, h))
    flag = lambda array: pl.BlockSpec(array.shape, lambda h: (0, 0))
    keys = sum(array.shape[0] for array in rows[1:]) // 2
    tokens = rows[0].shape[0]
    return pl.pallas_call(
        kernel,
        grid=(width // HD,),
        out_shape=jax.ShapeDtypeStruct((tokens, width), jnp.bfloat16),
        in_specs=[spec(array) for array in rows] + [flag(array) for array in masks],
        out_specs=pl.BlockSpec((tokens, HD), lambda h: (0, h)),
        cost_estimate=pl.CostEstimate(
            flops=4 * tokens * keys * width,
            bytes_accessed=4 * (tokens + keys) * width,
            transcendentals=tokens * keys * width // HD,
        ),
    )(*rows, *masks)


MESH = pl.DeviceIdType.MESH


def exchange_kernel(
    layers,
    key_ref,
    value_ref,
    count_ref,
    square_ref,
    weight_ref,
    key_out,
    value_out,
    count_out,
    square_out,
    weight_out,
    page_send,
    page_recv,
    tp_send,
    tp_recv,
    local_sem,
    right_recv,
    left_recv,
    row_recv,
    core_recv,
    weight_send,
):
    peer_count = 4 * layers
    req, tp = lax.axis_index("req"), lax.axis_index("tp")
    tp_count = square_out.shape[0]
    half, layer, core = req // (2 * layers), (req // 2) % layers, req % 2

    def place(h, z, c):
        return (h * layers + z) * 2 + c

    barrier = pltpu.get_barrier_semaphore()

    @pl.loop(1, peer_count)
    def _(i):
        pl.semaphore_signal(
            barrier, inc=1, device_id=((req + i) % peer_count, tp), device_id_type=MESH
        )

    @pl.loop(1, tp_count)
    def _(i):
        pl.semaphore_signal(
            barrier, inc=1, device_id=(req, (tp + i) % tp_count), device_id_type=MESH
        )

    locals_ = [
        pltpu.make_async_copy(key_ref.at[req], key_out.at[req], local_sem.at[0]),
        pltpu.make_async_copy(value_ref.at[req], value_out.at[req], local_sem.at[1]),
        pltpu.make_async_copy(count_ref.at[req], count_out.at[req], local_sem.at[2]),
        pltpu.make_async_copy(square_ref, square_out.at[tp], local_sem.at[3]),
        pltpu.make_async_copy(weight_ref, weight_out.at[req], local_sem.at[4]),
    ]
    for copy in locals_:
        copy.start()
    pl.semaphore_wait(barrier, peer_count + tp_count - 2)

    @pl.loop(1, tp_count)
    def _(i):
        pltpu.make_async_remote_copy(
            src_ref=square_ref,
            dst_ref=square_out.at[tp],
            send_sem=tp_send,
            recv_sem=tp_recv,
            device_id=(req, (tp + i) % tp_count),
            device_id_type=MESH,
        ).start()

    def send_weight(source, origin, target, recv_sem):
        pltpu.make_async_remote_copy(
            src_ref=source,
            dst_ref=weight_out.at[origin],
            send_sem=weight_send,
            recv_sem=recv_sem,
            device_id=(target, tp),
            device_id_type=MESH,
        ).start()

    def wait_block(sem):
        pltpu.make_async_copy(weight_out.at[0], weight_out.at[0], sem).wait()

    right = place(half, (layer + 1) % layers, core)
    left = place(half, (layer + layers - 1) % layers, core)
    across = place((half + 1) % 2, layer, core)
    beside = place(half, layer, (core + 1) % 2)

    def send_pages(target):
        for src, dst, sem in (
            (key_ref, key_out, 0),
            (value_ref, value_out, 1),
            (count_ref, count_out, 2),
        ):
            pltpu.make_async_remote_copy(
                src_ref=src.at[target],
                dst_ref=dst.at[req],
                send_sem=page_send.at[sem],
                recv_sem=page_recv.at[sem],
                device_id=(target, tp),
                device_id_type=MESH,
            ).start()

    def batch(k):
        shift = layers // 2 - (k + 1) // 2
        z = (layer + layers + shift * (2 * (k % 2) - 1)) % layers
        for h in range(2):
            for c in range(2):
                send_pages(place((half + h) % 2, z, (core + c) % 2))

    send_weight(weight_ref, req, right, right_recv.at[0])
    send_weight(weight_ref, req, left, left_recv.at[0])
    send_weight(weight_ref, req, across, row_recv.at[layer])
    send_weight(weight_ref, req, beside, core_recv)
    right_steps = layers // 2
    left_steps = layers - 1 - right_steps
    batch(0)

    def step(s, from_left, from_right):
        if from_left is not None:
            z = (layer + layers - 1 - s) % layers
            origin = place(half, z, core)
            wait_block(right_recv.at[s])
            if from_left:
                send_weight(weight_out.at[origin], origin, right, right_recv.at[s + 1])
            send_weight(weight_out.at[origin], origin, across, row_recv.at[z])
            send_weight(weight_out.at[origin], origin, beside, core_recv)
        if from_right is not None:
            z = (layer + 1 + s) % layers
            origin = place(half, z, core)
            wait_block(left_recv.at[s])
            if from_right:
                send_weight(weight_out.at[origin], origin, left, left_recv.at[s + 1])
            send_weight(weight_out.at[origin], origin, across, row_recv.at[z])
            send_weight(weight_out.at[origin], origin, beside, core_recv)
        batch(s + 1)

    @pl.loop(0, left_steps - 1)
    def _(s):
        step(s, True, True)

    for s in range(left_steps - 1, right_steps):
        step(s, s < right_steps - 1, s < left_steps - 1 if s < left_steps else None)

    @pl.loop(right_steps + 1, layers - 1)
    def _(k):
        batch(k)

    for h, c in ((0, 1), (1, 0), (1, 1)):
        send_pages(place((half + h) % 2, layer, (core + c) % 2))

    @pl.loop(0, layers)
    def _(s):
        z = (layer + layers + ((s + 1) // 2) * (2 * (s % 2) - 1)) % layers
        origin = place((half + 1) % 2, z, core)
        wait_block(row_recv.at[z])
        send_weight(weight_out.at[origin], origin, beside, core_recv)

    for copy in locals_:
        copy.wait()
    halves = weight_out.at[pl.ds(0, 2 * layers)]
    pltpu.make_async_copy(halves, halves, core_recv).wait()
    sent = weight_out.at[pl.ds(0, 4 * layers - 1)]
    pltpu.make_async_copy(sent, sent, weight_send).wait()
    for sem, out in ((0, key_out), (1, value_out), (2, count_out)):
        others = out.at[pl.ds(0, peer_count - 1)]
        pltpu.make_async_copy(others, others, page_recv.at[sem]).wait()
        pltpu.make_async_copy(others, others, page_send.at[sem]).wait()
    others = square_out.at[pl.ds(0, tp_count - 1)]
    pltpu.make_async_copy(others, others, tp_recv).wait()
    pltpu.make_async_copy(others, others, tp_send).wait()


def exchange(keys, values, counts, squares, weight, tp_count):
    peer_count = keys.shape[0]
    layers = peer_count // 4
    anywhere = pl.BlockSpec(memory_space=pl.ANY)
    shape = jax.ShapeDtypeStruct
    return pl.pallas_call(
        functools.partial(exchange_kernel, layers),
        out_shape=(
            shape(keys.shape, keys.dtype),
            shape(values.shape, values.dtype),
            shape(counts.shape, counts.dtype),
            shape((tp_count,) + squares.shape, squares.dtype),
            shape((peer_count,) + weight.shape, weight.dtype),
        ),
        in_specs=[anywhere] * 5,
        out_specs=(anywhere,) * 5,
        scratch_shapes=[
            pltpu.SemaphoreType.DMA((3,)),
            pltpu.SemaphoreType.DMA((3,)),
            pltpu.SemaphoreType.DMA,
            pltpu.SemaphoreType.DMA,
            pltpu.SemaphoreType.DMA((5,)),
            pltpu.SemaphoreType.DMA((layers,)),
            pltpu.SemaphoreType.DMA((layers,)),
            pltpu.SemaphoreType.DMA((layers,)),
            pltpu.SemaphoreType.DMA,
            pltpu.SemaphoreType.DMA,
        ],
        compiler_params=pltpu.CompilerParams(collective_id=0, has_side_effects=True),
    )(keys, values, counts, squares, weight)


def shards(
    queries,
    new_keys,
    new_values,
    query_gain,
    key_gain,
    cache_keys,
    cache_values,
    page_table,
    cache_lens,
    mig_pages,
    mig_dest,
    cross_queries,
    text_keys,
    text_values,
    out_weight,
    residual,
    gate,
    shift,
    scale,
):
    token_count, local_width = queries.shape
    tp_count = lax.axis_size("tp")
    full_width = local_width * tp_count
    peer_count = lax.axis_size("req")
    page_len = cache_keys.shape[1]
    peers = jnp.arange(peer_count, dtype=jnp.int32)

    destination = mig_dest[:, 0]
    slot_match = (destination[:, None] == peers[None, :]).astype(jnp.int32)
    position = jnp.sum(jnp.cumsum(slot_match, axis=0) * slot_match, axis=1) - 1
    target_slot = destination * CAP + position
    selection = jnp.arange(peer_count * CAP, dtype=jnp.int32)[:, None] == target_slot[None, :]
    slot_page = jnp.sum(jnp.where(selection, mig_pages, 0), axis=1)
    sent_keys = cache_keys[slot_page].reshape(peer_count, CAP * page_len, local_width)
    sent_values = cache_values[slot_page].reshape(peer_count, CAP * page_len, local_width)
    sent_counts = jnp.broadcast_to(
        jnp.sum(slot_match, axis=0)[:, None, None], (peer_count, 1, HD)
    )
    query_float = queries.astype(jnp.float32)
    key_float = new_keys.astype(jnp.float32)
    local_squares = jnp.stack(
        [jnp.sum(query_float * query_float, axis=1), jnp.sum(key_float * key_float, axis=1)]
    )
    arrived_keys, arrived_values, arrivals, all_squares, whole_weight = exchange(
        sent_keys, sent_values, sent_counts, local_squares[:, None, :], out_weight.T, tp_count
    )
    filled = arrivals[:, 0, :1] > jnp.arange(CAP, dtype=jnp.int32)[None, :]
    arrived_usable = jnp.broadcast_to(
        filled[:, :, None].astype(jnp.float32), (peer_count, CAP, page_len)
    ).reshape(1, -1)
    query_squares, key_squares = jnp.sum(all_squares[:, :, 0, :], axis=0)
    query_normed = (
        query_float * lax.rsqrt(query_squares / full_width + EPS)[:, None] * query_gain
    ).astype(jnp.bfloat16)
    key_normed = (key_float * lax.rsqrt(key_squares / full_width + EPS)[:, None] * key_gain).astype(
        jnp.bfloat16
    )
    own_pages = page_table[0]
    resident_keys = cache_keys[own_pages].reshape(-1, local_width)
    resident_values = cache_values[own_pages].reshape(-1, local_width)
    resident_usable = (
        jnp.arange(resident_keys.shape[0], dtype=jnp.int32) < cache_lens[0]
    ).astype(jnp.float32)[None, :]

    cross_out = per_head(cross_kernel, (cross_queries, text_keys, text_values), (), local_width)
    attended = per_head(
        self_kernel,
        (
            query_normed,
            resident_keys,
            resident_values,
            arrived_keys.reshape(-1, local_width),
            arrived_values.reshape(-1, local_width),
            key_normed,
            new_values,
        ),
        (resident_usable, arrived_usable),
        local_width,
    )
    partial_rows = lax.dot_general(
        attended,
        whole_weight.reshape(full_width, local_width),
        (((1,), (1,)), ((), ())),
        preferred_element_type=jnp.float32,
    ).astype(jnp.bfloat16)
    pieces = lax.all_to_all(
        jnp.stack(jnp.split(partial_rows, tp_count, axis=1)),
        "tp",
        split_axis=0,
        concat_axis=0,
        tiled=True,
    )
    projected = jnp.sum(pieces.astype(jnp.float32), axis=0)
    updated = residual.astype(jnp.float32) + gate.astype(jnp.float32) * projected
    local_mean = jnp.mean(updated, axis=1)
    local_var = jnp.mean(jnp.square(updated - local_mean[:, None]), axis=1)
    means, variances = lax.all_gather(jnp.stack([local_mean, local_var]), "tp", axis=1)
    row_mean = jnp.mean(means, axis=0)
    row_var = jnp.mean(variances + jnp.square(means - row_mean[None, :]), axis=0)
    stream = updated.astype(jnp.bfloat16)
    normed = (
        (updated - row_mean[:, None])
        * lax.rsqrt(row_var + EPS)[:, None]
        * (1.0 + scale.astype(jnp.float32))
        + shift.astype(jnp.float32)
    ).astype(jnp.bfloat16)
    return (stream, normed, cross_out)


def solution(mesh):
    in_specs = (
        P("req", "tp"),
        P("req", "tp"),
        P("req", "tp"),
        P("tp"),
        P("tp"),
        P("req", None, "tp"),
        P("req", None, "tp"),
        P("req", None),
        P("req"),
        P("req", None),
        P("req", None),
        P("req", "tp"),
        P("req", "tp"),
        P("req", "tp"),
        P("tp", "req"),
        P("req", "tp"),
        P("req", "tp"),
        P("req", "tp"),
        P("req", "tp"),
    )
    out_specs = (P("req", "tp"), P("req", "tp"), P("req", "tp"))
    return jax.shard_map(shards, mesh=mesh, in_specs=in_specs, out_specs=out_specs, check_vma=False)
```

```python
import functools
import math

import jax
import jax.numpy as jnp
from jax import lax
from jax.experimental import pallas as pl
from jax.experimental.pallas import tpu as pltpu
from jax.sharding import PartitionSpec as P

HD = 128
CAP = 2


EPS = 1e-06


def head_scores(query, keys, scale):
    return (
        lax.dot_general(query, keys, (((1,), (1,)), ((), ())), preferred_element_type=jnp.float32)
        * scale
    )


def self_kernel(q_ref, kr_ref, vr_ref, ka_ref, va_ref, kn_ref, vn_ref, ur_ref, ua_ref, o_ref):
    scale = 1.0 / math.sqrt(HD)
    query = q_ref[...]
    resident = jnp.where(ur_ref[...] > 0, head_scores(query, kr_ref[...], scale), -jnp.inf)
    arrived = jnp.where(ua_ref[...] > 0, head_scores(query, ka_ref[...], scale), -jnp.inf)
    own = head_scores(query, kn_ref[...], scale)
    row_max = jnp.maximum(
        jnp.max(own, axis=1, keepdims=True),
        jnp.maximum(
            jnp.max(resident, axis=1, keepdims=True), jnp.max(arrived, axis=1, keepdims=True)
        ),
    )
    denominator = jnp.zeros_like(row_max)
    mixed = jnp.zeros(o_ref.shape, jnp.float32)
    for scores, values in ((resident, vr_ref), (arrived, va_ref), (own, vn_ref)):
        exponent = jnp.exp(scores - row_max)
        denominator += jnp.sum(exponent, axis=1, keepdims=True)
        mixed += jnp.dot(
            exponent.astype(jnp.bfloat16), values[...], preferred_element_type=jnp.float32
        )
    o_ref[...] = (mixed / denominator).astype(jnp.bfloat16)


def cross_kernel(q_ref, k_ref, v_ref, o_ref):
    scores = head_scores(q_ref[...], k_ref[...], 1.0 / math.sqrt(HD))
    exponent = jnp.exp(scores - jnp.max(scores, axis=1, keepdims=True))
    denominator = jnp.sum(exponent, axis=1, keepdims=True)
    mixed = jnp.dot(exponent.astype(jnp.bfloat16), v_ref[...], preferred_element_type=jnp.float32)
    o_ref[...] = (mixed / denominator).astype(jnp.bfloat16)


def per_head(kernel, rows, masks, width):
    spec = lambda array: pl.BlockSpec((array.shape[0], HD), lambda h: (0, h))
    flag = lambda array: pl.BlockSpec(array.shape, lambda h: (0, 0))
    keys = sum(array.shape[0] for array in rows[1:]) // 2
    tokens = rows[0].shape[0]
    return pl.pallas_call(
        kernel,
        grid=(width // HD,),
        out_shape=jax.ShapeDtypeStruct((tokens, width), jnp.bfloat16),
        in_specs=[spec(array) for array in rows] + [flag(array) for array in masks],
        out_specs=pl.BlockSpec((tokens, HD), lambda h: (0, h)),
        cost_estimate=pl.CostEstimate(
            flops=4 * tokens * keys * width,
            bytes_accessed=4 * (tokens + keys) * width,
            transcendentals=tokens * keys * width // HD,
        ),
    )(*rows, *masks)


MESH = pl.DeviceIdType.MESH


def exchange_kernel(
    layers,
    key_ref,
    value_ref,
    count_ref,
    square_ref,
    weight_ref,
    cross_query_ref,
    text_key_ref,
    text_value_ref,
    key_out,
    value_out,
    count_out,
    square_out,
    weight_out,
    cross_ref,
    page_send,
    page_recv,
    tp_send,
    tp_recv,
    local_sem,
    right_recv,
    left_recv,
    row_recv,
    core_recv,
    weight_send,
):
    peer_count = 4 * layers
    req, tp = lax.axis_index("req"), lax.axis_index("tp")
    tp_count = square_out.shape[0]
    half, layer, core = req // (2 * layers), (req // 2) % layers, req % 2

    def place(h, z, c):
        return (h * layers + z) * 2 + c

    barrier = pltpu.get_barrier_semaphore()

    @pl.loop(1, peer_count)
    def _(i):
        pl.semaphore_signal(
            barrier, inc=1, device_id=((req + i) % peer_count, tp), device_id_type=MESH
        )

    @pl.loop(1, tp_count)
    def _(i):
        pl.semaphore_signal(
            barrier, inc=1, device_id=(req, (tp + i) % tp_count), device_id_type=MESH
        )

    locals_ = [
        pltpu.make_async_copy(key_ref.at[req], key_out.at[req], local_sem.at[0]),
        pltpu.make_async_copy(value_ref.at[req], value_out.at[req], local_sem.at[1]),
        pltpu.make_async_copy(count_ref.at[req], count_out.at[req], local_sem.at[2]),
        pltpu.make_async_copy(square_ref, square_out.at[tp], local_sem.at[3]),
        pltpu.make_async_copy(weight_ref, weight_out.at[req], local_sem.at[4]),
    ]
    for copy in locals_:
        copy.start()
    pl.semaphore_wait(barrier, peer_count + tp_count - 2)

    @pl.loop(1, tp_count)
    def _(i):
        pltpu.make_async_remote_copy(
            src_ref=square_ref,
            dst_ref=square_out.at[tp],
            send_sem=tp_send,
            recv_sem=tp_recv,
            device_id=(req, (tp + i) % tp_count),
            device_id_type=MESH,
        ).start()

    def send_weight(source, origin, target, recv_sem):
        pltpu.make_async_remote_copy(
            src_ref=source,
            dst_ref=weight_out.at[origin],
            send_sem=weight_send,
            recv_sem=recv_sem,
            device_id=(target, tp),
            device_id_type=MESH,
        ).start()

    def wait_block(sem):
        pltpu.make_async_copy(weight_out.at[0], weight_out.at[0], sem).wait()

    right = place(half, (layer + 1) % layers, core)
    left = place(half, (layer + layers - 1) % layers, core)
    across = place((half + 1) % 2, layer, core)
    beside = place(half, layer, (core + 1) % 2)

    def send_pages(target):
        for src, dst, sem in (
            (key_ref, key_out, 0),
            (value_ref, value_out, 1),
            (count_ref, count_out, 2),
        ):
            pltpu.make_async_remote_copy(
                src_ref=src.at[target],
                dst_ref=dst.at[req],
                send_sem=page_send.at[sem],
                recv_sem=page_recv.at[sem],
                device_id=(target, tp),
                device_id_type=MESH,
            ).start()

    def batch(k):
        shift = layers // 2 - (k + 1) // 2
        z = (layer + layers + shift * (2 * (k % 2) - 1)) % layers
        for h in range(2):
            for c in range(2):
                send_pages(place((half + h) % 2, z, (core + c) % 2))

    send_weight(weight_ref, req, right, right_recv.at[0])
    send_weight(weight_ref, req, left, left_recv.at[0])
    send_weight(weight_ref, req, across, row_recv.at[layer])
    send_weight(weight_ref, req, beside, core_recv)
    right_steps = layers // 2
    left_steps = layers - 1 - right_steps
    batch(0)

    def step(s, from_left, from_right):
        if from_left is not None:
            z = (layer + layers - 1 - s) % layers
            origin = place(half, z, core)
            wait_block(right_recv.at[s])
            if from_left:
                send_weight(weight_out.at[origin], origin, right, right_recv.at[s + 1])
            send_weight(weight_out.at[origin], origin, across, row_recv.at[z])
            send_weight(weight_out.at[origin], origin, beside, core_recv)
        if from_right is not None:
            z = (layer + 1 + s) % layers
            origin = place(half, z, core)
            wait_block(left_recv.at[s])
            if from_right:
                send_weight(weight_out.at[origin], origin, left, left_recv.at[s + 1])
            send_weight(weight_out.at[origin], origin, across, row_recv.at[z])
            send_weight(weight_out.at[origin], origin, beside, core_recv)
        batch(s + 1)

    @pl.loop(0, left_steps - 1)
    def _(s):
        step(s, True, True)

    for s in range(left_steps - 1, right_steps):
        step(s, s < right_steps - 1, s < left_steps - 1 if s < left_steps else None)

    @pl.loop(right_steps + 1, layers - 1)
    def _(k):
        batch(k)

    for h, c in ((0, 1), (1, 0), (1, 1)):
        send_pages(place((half + h) % 2, layer, (core + c) % 2))

    @pl.loop(0, layers)
    def _(s):
        z = (layer + layers + ((s + 1) // 2) * (2 * (s % 2) - 1)) % layers
        origin = place((half + 1) % 2, z, core)
        wait_block(row_recv.at[z])
        send_weight(weight_out.at[origin], origin, beside, core_recv)

    for head in range(cross_ref.shape[1] // HD):
        columns = pl.ds(head * HD, HD)
        cross_kernel(
            cross_query_ref.at[:, columns],
            text_key_ref.at[:, columns],
            text_value_ref.at[:, columns],
            cross_ref.at[:, columns],
        )

    for copy in locals_:
        copy.wait()
    halves = weight_out.at[pl.ds(0, 2 * layers)]
    pltpu.make_async_copy(halves, halves, core_recv).wait()
    sent = weight_out.at[pl.ds(0, 4 * layers - 1)]
    pltpu.make_async_copy(sent, sent, weight_send).wait()
    for sem, out in ((0, key_out), (1, value_out), (2, count_out)):
        others = out.at[pl.ds(0, peer_count - 1)]
        pltpu.make_async_copy(others, others, page_recv.at[sem]).wait()
        pltpu.make_async_copy(others, others, page_send.at[sem]).wait()
    others = square_out.at[pl.ds(0, tp_count - 1)]
    pltpu.make_async_copy(others, others, tp_recv).wait()
    pltpu.make_async_copy(others, others, tp_send).wait()


def exchange(keys, values, counts, squares, weight, cross, tp_count):
    peer_count = keys.shape[0]
    layers = peer_count // 4
    anywhere = pl.BlockSpec(memory_space=pl.ANY)
    vmem = pl.BlockSpec(memory_space=pltpu.VMEM)
    shape = jax.ShapeDtypeStruct
    return pl.pallas_call(
        functools.partial(exchange_kernel, layers),
        out_shape=(
            shape(keys.shape, keys.dtype),
            shape(values.shape, values.dtype),
            shape(counts.shape, counts.dtype),
            shape((tp_count,) + squares.shape, squares.dtype),
            shape((peer_count,) + weight.shape, weight.dtype),
            shape(cross[0].shape, cross[0].dtype),
        ),
        in_specs=[anywhere] * 5 + [vmem] * 3,
        out_specs=(anywhere,) * 5 + (vmem,),
        scratch_shapes=[
            pltpu.SemaphoreType.DMA((3,)),
            pltpu.SemaphoreType.DMA((3,)),
            pltpu.SemaphoreType.DMA,
            pltpu.SemaphoreType.DMA,
            pltpu.SemaphoreType.DMA((5,)),
            pltpu.SemaphoreType.DMA((layers,)),
            pltpu.SemaphoreType.DMA((layers,)),
            pltpu.SemaphoreType.DMA((layers,)),
            pltpu.SemaphoreType.DMA,
            pltpu.SemaphoreType.DMA,
        ],
        compiler_params=pltpu.CompilerParams(collective_id=0, has_side_effects=True),
    )(keys, values, counts, squares, weight, *cross)


def project_kernel(
    attended_ref,
    weight_ref,
    residual_ref,
    gate_ref,
    shift_ref,
    scale_ref,
    stream_ref,
    normed_ref,
    far,
    to_right,
    to_left,
    relay_right,
    relay_left,
    from_left,
    from_right,
    own,
    to_row,
    from_row,
    stat_out,
    stat_in,
    send_sem,
    recv_sem,
    stat_sem,
):
    req, tp = lax.axis_index("req"), lax.axis_index("tp")
    tp_count = stat_in.shape[0]
    ring = tp_count // 2
    row, x = tp // ring, tp % ring
    tokens, width = residual_ref.shape
    part = tokens // 2

    barrier = pltpu.get_barrier_semaphore()
    for i in range(1, tp_count):
        pl.semaphore_signal(
            barrier, inc=1, device_id=(req, (tp + i) % tp_count), device_id_type=MESH
        )

    right = row * ring + (x + 1) % ring
    left = row * ring + (x + ring - 1) % ring
    other = ((row + 1) % 2) * ring + x

    def send(src, dst, sem, target):
        copy = pltpu.make_async_remote_copy(
            src_ref=src,
            dst_ref=dst,
            send_sem=send_sem.at[sem],
            recv_sem=recv_sem.at[sem],
            device_id=(req, target),
            device_id_type=MESH,
        )
        copy.start()
        return copy

    def block(shift, j):
        owner = ((row + j) % 2) * ring + (x + shift) % ring
        rows = weight_ref[pl.ds(pl.multiple_of(owner * width, width), width), :]
        return lax.dot_general(
            attended_ref[...],
            rows,
            (((1,), (1,)), ((), ())),
            preferred_element_type=jnp.float32,
        ).astype(jnp.bfloat16)

    for j in range(2):
        product = block(2, j)
        for p in range(2):
            far[p, j] = product[p * part : (p + 1) * part]
    pl.semaphore_wait(barrier, tp_count - 1)
    copies = [send(far.at[0], relay_right, 0, right), send(far.at[1], relay_left, 1, left)]
    for j in range(2):
        product = block(1, j)
        for p in range(2):
            to_right[p, j] = product[p * part : (p + 1) * part]
    copies.append(send(to_right.at[1], from_left.at[1], 2, right))
    for j in range(2):
        product = block(ring - 1, j)
        for p in range(2):
            to_left[p, j] = product[p * part : (p + 1) * part]
    copies.append(send(to_left.at[0], from_right.at[0], 3, left))
    for j in range(2):
        product = block(0, j)
        for p in range(2):
            own[p, j] = product[p * part : (p + 1) * part]

    def total(*terms):
        return functools.reduce(jnp.add, [term.astype(jnp.float32) for term in terms])

    copies[0].wait_recv()
    for j in range(2):
        to_right[0, j] = total(to_right[0, j], relay_right[j]).astype(jnp.bfloat16)
    copies.append(send(to_right.at[0], from_left.at[0], 4, right))
    copies[1].wait_recv()
    for j in range(2):
        to_left[1, j] = total(to_left[1, j], relay_left[j]).astype(jnp.bfloat16)
    copies.append(send(to_left.at[1], from_right.at[1], 5, left))
    copies[2].wait_recv()
    copies[3].wait_recv()
    for p in range(2):
        copies[4 + p].wait_recv()
        to_row[p] = total(own[p, 1], from_left[p, 1], from_right[p, 1]).astype(jnp.bfloat16)
        copies.append(send(to_row.at[p], from_row.at[p], 6 + p, other))

    updated = []
    for p in range(2):
        local = total(own[p, 0], from_left[p, 0], from_right[p, 0])
        copies[6 + p].wait_recv()
        span = pl.ds(p * part, part)
        value = residual_ref[span, :].astype(jnp.float32) + gate_ref[...].astype(jnp.float32) * (
            local + from_row[p].astype(jnp.float32)
        )
        stream_ref[span, :] = value.astype(jnp.bfloat16)
        mean = jnp.sum(value, axis=1, keepdims=True) / width
        variance = jnp.sum(jnp.square(value - mean), axis=1, keepdims=True) / width
        lane = lax.broadcasted_iota(jnp.int32, (part, HD), 1)
        packed = jnp.where(lane == 0, mean, jnp.where(lane == 1, variance, 0.0))
        stat_out[p] = jnp.transpose(packed)[0:8]
        updated.append(value)

    stat_in[tp] = stat_out[...]
    for i in range(1, tp_count):
        copy = pltpu.make_async_remote_copy(
            src_ref=stat_out,
            dst_ref=stat_in.at[tp],
            send_sem=stat_sem.at[0],
            recv_sem=stat_sem.at[1],
            device_id=(req, (tp + i) % tp_count),
            device_id_type=MESH,
        )
        copy.start()
    others = stat_in.at[pl.ds(0, tp_count - 1)]
    pltpu.make_async_copy(others, others, stat_sem.at[1]).wait()
    for p in range(2):
        arrived = [stat_in[i, p] for i in range(tp_count)]
        row_mean = functools.reduce(jnp.add, [a[0:1] for a in arrived]) / tp_count
        row_var = (
            functools.reduce(
                jnp.add, [a[1:2] + jnp.square(a[0:1] - row_mean) for a in arrived]
            )
            / tp_count
        )
        line = lax.broadcasted_iota(jnp.int32, (HD, part), 0)
        packed = jnp.transpose(
            jnp.where(line == 0, row_mean, jnp.where(line == 1, lax.rsqrt(row_var + EPS), 0.0))
        )
        normed = (updated[p] - packed[:, 0:1]) * packed[:, 1:2] * (
            1.0 + scale_ref[...].astype(jnp.float32)
        ) + shift_ref[...].astype(jnp.float32)
        normed_ref[pl.ds(p * part, part), :] = normed.astype(jnp.bfloat16)
    for copy in copies:
        copy.wait_send()
    pltpu.make_async_copy(others, others, stat_sem.at[0]).wait()


def project(attended, weight, residual, gate, shift, scale, tp_count):
    tokens, width = residual.shape
    part = tokens // 2
    vmem = pl.BlockSpec(memory_space=pltpu.VMEM)
    pair = pltpu.VMEM((2, part, width), jnp.bfloat16)
    quad = pltpu.VMEM((2, 2, part, width), jnp.bfloat16)
    stat = pltpu.VMEM((2, 8, part), jnp.float32)
    return pl.pallas_call(
        project_kernel,
        out_shape=(jax.ShapeDtypeStruct(residual.shape, jnp.bfloat16),) * 2,
        in_specs=[vmem] * 6,
        out_specs=(vmem, vmem),
        scratch_shapes=[
            quad,
            quad,
            quad,
            pair,
            pair,
            quad,
            quad,
            quad,
            pair,
            pair,
            stat,
            pltpu.VMEM((tp_count, 2, 8, part), jnp.float32),
            pltpu.SemaphoreType.DMA((8,)),
            pltpu.SemaphoreType.DMA((8,)),
            pltpu.SemaphoreType.DMA((2,)),
        ],
        compiler_params=pltpu.CompilerParams(collective_id=1, has_side_effects=True),
    )(attended, weight, residual, gate, shift, scale)


def shards(
    queries,
    new_keys,
    new_values,
    query_gain,
    key_gain,
    cache_keys,
    cache_values,
    page_table,
    cache_lens,
    mig_pages,
    mig_dest,
    cross_queries,
    text_keys,
    text_values,
    out_weight,
    residual,
    gate,
    shift,
    scale,
):
    token_count, local_width = queries.shape
    tp_count = lax.axis_size("tp")
    full_width = local_width * tp_count
    peer_count = lax.axis_size("req")
    page_len = cache_keys.shape[1]
    peers = jnp.arange(peer_count, dtype=jnp.int32)

    destination = mig_dest[:, 0]
    slot_match = (destination[:, None] == peers[None, :]).astype(jnp.int32)
    position = jnp.sum(jnp.cumsum(slot_match, axis=0) * slot_match, axis=1) - 1
    target_slot = destination * CAP + position
    selection = jnp.arange(peer_count * CAP, dtype=jnp.int32)[:, None] == target_slot[None, :]
    slot_page = jnp.sum(jnp.where(selection, mig_pages, 0), axis=1)
    sent_keys = cache_keys[slot_page].reshape(peer_count, CAP * page_len, local_width)
    sent_values = cache_values[slot_page].reshape(peer_count, CAP * page_len, local_width)
    sent_counts = jnp.broadcast_to(
        jnp.sum(slot_match, axis=0)[:, None, None], (peer_count, 1, HD)
    )
    query_float = queries.astype(jnp.float32)
    key_float = new_keys.astype(jnp.float32)
    local_squares = jnp.stack(
        [jnp.sum(query_float * query_float, axis=1), jnp.sum(key_float * key_float, axis=1)]
    )
    arrived_keys, arrived_values, arrivals, all_squares, whole_weight, cross_out = exchange(
        sent_keys,
        sent_values,
        sent_counts,
        local_squares[:, None, :],
        out_weight.T,
        (cross_queries, text_keys, text_values),
        tp_count,
    )
    filled = arrivals[:, 0, :1] > jnp.arange(CAP, dtype=jnp.int32)[None, :]
    arrived_usable = jnp.broadcast_to(
        filled[:, :, None].astype(jnp.float32), (peer_count, CAP, page_len)
    ).reshape(1, -1)
    query_squares, key_squares = jnp.sum(all_squares[:, :, 0, :], axis=0)
    query_normed = (
        query_float * lax.rsqrt(query_squares / full_width + EPS)[:, None] * query_gain
    ).astype(jnp.bfloat16)
    key_normed = (key_float * lax.rsqrt(key_squares / full_width + EPS)[:, None] * key_gain).astype(
        jnp.bfloat16
    )
    own_pages = page_table[0]
    resident_keys = cache_keys[own_pages].reshape(-1, local_width)
    resident_values = cache_values[own_pages].reshape(-1, local_width)
    resident_usable = (
        jnp.arange(resident_keys.shape[0], dtype=jnp.int32) < cache_lens[0]
    ).astype(jnp.float32)[None, :]

    attended = per_head(
        self_kernel,
        (
            query_normed,
            resident_keys,
            resident_values,
            arrived_keys.reshape(-1, local_width),
            arrived_values.reshape(-1, local_width),
            key_normed,
            new_values,
        ),
        (resident_usable, arrived_usable),
        local_width,
    )
    stream, normed = project(
        attended,
        whole_weight.reshape(full_width, local_width),
        residual,
        gate,
        shift,
        scale,
        tp_count,
    )
    return (stream, normed, cross_out)


def solution(mesh):
    in_specs = (
        P("req", "tp"),
        P("req", "tp"),
        P("req", "tp"),
        P("tp"),
        P("tp"),
        P("req", None, "tp"),
        P("req", None, "tp"),
        P("req", None),
        P("req"),
        P("req", None),
        P("req", None),
        P("req", "tp"),
        P("req", "tp"),
        P("req", "tp"),
        P("tp", "req"),
        P("req", "tp"),
        P("req", "tp"),
        P("req", "tp"),
        P("req", "tp"),
    )
    out_specs = (P("req", "tp"), P("req", "tp"), P("req", "tp"))
    return jax.shard_map(shards, mesh=mesh, in_specs=in_specs, out_specs=out_specs, check_vma=False)
```

```python
import functools
import math

import jax
import jax.numpy as jnp
from jax import lax
from jax.experimental import pallas as pl
from jax.experimental.pallas import tpu as pltpu
from jax.sharding import PartitionSpec as P

HD = 128
CAP = 2


EPS = 1e-06


def head_scores(query, keys, scale):
    return (
        lax.dot_general(query, keys, (((1,), (1,)), ((), ())), preferred_element_type=jnp.float32)
        * scale
    )


def self_kernel(q_ref, kr_ref, vr_ref, ka_ref, va_ref, kn_ref, vn_ref, ur_ref, ua_ref, o_ref):
    scale = 1.0 / math.sqrt(HD)
    query = q_ref[...]
    resident = jnp.where(ur_ref[...] > 0, head_scores(query, kr_ref[...], scale), -jnp.inf)
    arrived = jnp.where(ua_ref[...] > 0, head_scores(query, ka_ref[...], scale), -jnp.inf)
    own = head_scores(query, kn_ref[...], scale)
    row_max = jnp.maximum(
        jnp.max(own, axis=1, keepdims=True),
        jnp.maximum(
            jnp.max(resident, axis=1, keepdims=True), jnp.max(arrived, axis=1, keepdims=True)
        ),
    )
    denominator = jnp.zeros_like(row_max)
    mixed = jnp.zeros(o_ref.shape, jnp.float32)
    for scores, values in ((resident, vr_ref), (arrived, va_ref), (own, vn_ref)):
        exponent = jnp.exp(scores - row_max)
        denominator += jnp.sum(exponent, axis=1, keepdims=True)
        mixed += jnp.dot(
            exponent.astype(jnp.bfloat16), values[...], preferred_element_type=jnp.float32
        )
    o_ref[...] = (mixed / denominator).astype(jnp.bfloat16)


def cross_kernel(q_ref, k_ref, v_ref, o_ref):
    scores = head_scores(q_ref[...], k_ref[...], 1.0 / math.sqrt(HD))
    exponent = jnp.exp(scores - jnp.max(scores, axis=1, keepdims=True))
    denominator = jnp.sum(exponent, axis=1, keepdims=True)
    mixed = jnp.dot(exponent.astype(jnp.bfloat16), v_ref[...], preferred_element_type=jnp.float32)
    o_ref[...] = (mixed / denominator).astype(jnp.bfloat16)


def per_head(kernel, rows, masks, width):
    spec = lambda array: pl.BlockSpec((array.shape[0], HD), lambda h: (0, h))
    flag = lambda array: pl.BlockSpec(array.shape, lambda h: (0, 0))
    keys = sum(array.shape[0] for array in rows[1:]) // 2
    tokens = rows[0].shape[0]
    return pl.pallas_call(
        kernel,
        grid=(width // HD,),
        out_shape=jax.ShapeDtypeStruct((tokens, width), jnp.bfloat16),
        in_specs=[spec(array) for array in rows] + [flag(array) for array in masks],
        out_specs=pl.BlockSpec((tokens, HD), lambda h: (0, h)),
        cost_estimate=pl.CostEstimate(
            flops=4 * tokens * keys * width,
            bytes_accessed=4 * (tokens + keys) * width,
            transcendentals=tokens * keys * width // HD,
        ),
    )(*rows, *masks)


MESH = pl.DeviceIdType.MESH


def exchange_kernel(
    layers,
    key_ref,
    value_ref,
    count_ref,
    square_ref,
    weight_ref,
    cross_query_ref,
    text_key_ref,
    text_value_ref,
    key_out,
    value_out,
    count_out,
    square_out,
    weight_out,
    cross_ref,
    page_send,
    page_recv,
    tp_send,
    tp_recv,
    local_sem,
    right_recv,
    left_recv,
    row_recv,
    core_recv,
    weight_send,
    relay,
    relay_send,
    relay_recv,
):
    peer_count = 4 * layers
    req, tp = lax.axis_index("req"), lax.axis_index("tp")
    tp_count = square_out.shape[0]
    half, layer, core = req // (2 * layers), (req // 2) % layers, req % 2

    def place(h, z, c):
        return (h * layers + z) * 2 + c

    barrier = pltpu.get_barrier_semaphore()

    @pl.loop(1, peer_count)
    def _(i):
        pl.semaphore_signal(
            barrier, inc=1, device_id=((req + i) % peer_count, tp), device_id_type=MESH
        )

    @pl.loop(1, tp_count)
    def _(i):
        pl.semaphore_signal(
            barrier, inc=1, device_id=(req, (tp + i) % tp_count), device_id_type=MESH
        )

    locals_ = [
        pltpu.make_async_copy(key_ref.at[req], key_out.at[req], local_sem.at[0]),
        pltpu.make_async_copy(value_ref.at[req], value_out.at[req], local_sem.at[1]),
        pltpu.make_async_copy(count_ref.at[req], count_out.at[req], local_sem.at[2]),
        pltpu.make_async_copy(square_ref, square_out.at[tp], local_sem.at[3]),
        pltpu.make_async_copy(weight_ref, weight_out.at[req], local_sem.at[4]),
    ]
    for copy in locals_:
        copy.start()
    pl.semaphore_wait(barrier, peer_count + tp_count - 2)

    @pl.loop(1, tp_count)
    def _(i):
        pltpu.make_async_remote_copy(
            src_ref=square_ref,
            dst_ref=square_out.at[tp],
            send_sem=tp_send,
            recv_sem=tp_recv,
            device_id=(req, (tp + i) % tp_count),
            device_id_type=MESH,
        ).start()

    def send_weight(source, origin, target, recv_sem):
        pltpu.make_async_remote_copy(
            src_ref=source,
            dst_ref=weight_out.at[origin],
            send_sem=weight_send,
            recv_sem=recv_sem,
            device_id=(target, tp),
            device_id_type=MESH,
        ).start()

    def wait_block(sem):
        pltpu.make_async_copy(weight_out.at[0], weight_out.at[0], sem).wait()

    right = place(half, (layer + 1) % layers, core)
    left = place(half, (layer + layers - 1) % layers, core)
    across = place((half + 1) % 2, layer, core)
    beside = place(half, layer, (core + 1) % 2)

    pages = ((key_ref, key_out, 0), (value_ref, value_out, 1))
    counts = (count_ref, count_out, 2)

    def send_pages(target, what):
        for src, dst, sem in what:
            pltpu.make_async_remote_copy(
                src_ref=src.at[target],
                dst_ref=dst.at[req],
                send_sem=page_send.at[sem],
                recv_sem=page_recv.at[sem],
                device_id=(target, tp),
                device_id_type=MESH,
            ).start()

    def batch(k):
        shift = layers // 2 - (k + 1) // 2
        z = (layer + layers + shift * (2 * (k % 2) - 1)) % layers
        for h in range(2):
            for c in range(2):
                send_pages(place((half + h) % 2, z, (core + c) % 2), (*pages, counts))

    opposite = (layer + layers // 2) % layers
    quarter = layers // 4

    def relayed(h):
        target = place((half + h) % 2, opposite, (core + 1) % 2)
        middle = place((half + h) % 2, (layer + layers - quarter) % layers, core)
        send_pages(target, (counts,))
        return [
            pltpu.make_async_remote_copy(
                src_ref=src.at[target],
                dst_ref=relay.at[h, sem],
                send_sem=relay_send.at[h, sem],
                recv_sem=relay_recv.at[h, sem],
                device_id=(middle, tp),
                device_id_type=MESH,
            )
            for src, _, sem in pages
        ]

    def pass_on(h):
        source = place((half + h) % 2, (layer + quarter) % layers, core)
        target = place(half, (layer + layers - quarter) % layers, (core + 1) % 2)
        for _, dst, sem in pages:
            pltpu.make_async_remote_copy(
                src_ref=relay.at[h, sem],
                dst_ref=dst.at[source],
                send_sem=page_send.at[sem],
                recv_sem=page_recv.at[sem],
                device_id=(target, tp),
                device_id_type=MESH,
            ).start()

    send_weight(weight_ref, req, right, right_recv.at[0])
    send_weight(weight_ref, req, left, left_recv.at[0])
    send_weight(weight_ref, req, across, row_recv.at[layer])
    send_weight(weight_ref, req, beside, core_recv)
    right_steps = layers // 2
    left_steps = layers - 1 - right_steps
    via = relayed(0) + relayed(1)
    for copy in via:
        copy.start()
    for h in range(2):
        send_pages(place((half + h) % 2, opposite, core), (*pages, counts))

    def step(s, from_left, from_right):
        if from_left is not None:
            z = (layer + layers - 1 - s) % layers
            origin = place(half, z, core)
            wait_block(right_recv.at[s])
            if from_left:
                send_weight(weight_out.at[origin], origin, right, right_recv.at[s + 1])
            send_weight(weight_out.at[origin], origin, across, row_recv.at[z])
            send_weight(weight_out.at[origin], origin, beside, core_recv)
        if from_right is not None:
            z = (layer + 1 + s) % layers
            origin = place(half, z, core)
            wait_block(left_recv.at[s])
            if from_right:
                send_weight(weight_out.at[origin], origin, left, left_recv.at[s + 1])
            send_weight(weight_out.at[origin], origin, across, row_recv.at[z])
            send_weight(weight_out.at[origin], origin, beside, core_recv)
        batch(s + 1)

    @pl.loop(0, left_steps - 1)
    def _(s):
        step(s, True, True)

    for s in range(left_steps - 1, right_steps):
        step(s, s < right_steps - 1, s < left_steps - 1 if s < left_steps else None)

    for copy in via:
        copy.wait_recv()
    for h in range(2):
        pass_on(h)

    @pl.loop(right_steps + 1, layers - 1)
    def _(k):
        batch(k)

    for h, c in ((0, 1), (1, 0), (1, 1)):
        send_pages(place((half + h) % 2, layer, (core + c) % 2), (*pages, counts))

    @pl.loop(0, layers)
    def _(s):
        z = (layer + layers + ((s + 1) // 2) * (2 * (s % 2) - 1)) % layers
        origin = place((half + 1) % 2, z, core)
        wait_block(row_recv.at[z])
        send_weight(weight_out.at[origin], origin, beside, core_recv)

    for head in range(cross_ref.shape[1] // HD):
        columns = pl.ds(head * HD, HD)
        cross_kernel(
            cross_query_ref.at[:, columns],
            text_key_ref.at[:, columns],
            text_value_ref.at[:, columns],
            cross_ref.at[:, columns],
        )

    for copy in locals_:
        copy.wait()
    halves = weight_out.at[pl.ds(0, 2 * layers)]
    pltpu.make_async_copy(halves, halves, core_recv).wait()
    sent = weight_out.at[pl.ds(0, 4 * layers - 1)]
    pltpu.make_async_copy(sent, sent, weight_send).wait()
    for sem, out in ((0, key_out), (1, value_out), (2, count_out)):
        others = out.at[pl.ds(0, peer_count - 1)]
        pltpu.make_async_copy(others, others, page_recv.at[sem]).wait()
        pltpu.make_async_copy(others, others, page_send.at[sem]).wait()
    for copy in via:
        copy.wait_send()
    others = square_out.at[pl.ds(0, tp_count - 1)]
    pltpu.make_async_copy(others, others, tp_recv).wait()
    pltpu.make_async_copy(others, others, tp_send).wait()


def exchange(keys, values, counts, squares, weight, cross, tp_count):
    peer_count = keys.shape[0]
    layers = peer_count // 4
    anywhere = pl.BlockSpec(memory_space=pl.ANY)
    vmem = pl.BlockSpec(memory_space=pltpu.VMEM)
    shape = jax.ShapeDtypeStruct
    return pl.pallas_call(
        functools.partial(exchange_kernel, layers),
        out_shape=(
            shape(keys.shape, keys.dtype),
            shape(values.shape, values.dtype),
            shape(counts.shape, counts.dtype),
            shape((tp_count,) + squares.shape, squares.dtype),
            shape((peer_count,) + weight.shape, weight.dtype),
            shape(cross[0].shape, cross[0].dtype),
        ),
        in_specs=[anywhere] * 5 + [vmem] * 3,
        out_specs=(anywhere,) * 5 + (vmem,),
        scratch_shapes=[
            pltpu.SemaphoreType.DMA((3,)),
            pltpu.SemaphoreType.DMA((3,)),
            pltpu.SemaphoreType.DMA,
            pltpu.SemaphoreType.DMA,
            pltpu.SemaphoreType.DMA((5,)),
            pltpu.SemaphoreType.DMA((layers,)),
            pltpu.SemaphoreType.DMA((layers,)),
            pltpu.SemaphoreType.DMA((layers,)),
            pltpu.SemaphoreType.DMA,
            pltpu.SemaphoreType.DMA,
            pltpu.VMEM((2, 2) + keys.shape[1:], keys.dtype),
            pltpu.SemaphoreType.DMA((2, 2)),
            pltpu.SemaphoreType.DMA((2, 2)),
        ],
        compiler_params=pltpu.CompilerParams(collective_id=0, has_side_effects=True),
    )(keys, values, counts, squares, weight, *cross)


def project_kernel(
    attended_ref,
    weight_ref,
    residual_ref,
    gate_ref,
    updated_ref,
    stat_ref,
    far,
    to_right,
    to_left,
    relay_right,
    relay_left,
    from_left,
    from_right,
    own,
    to_row,
    from_row,
    stat_out,
    stat_in,
    send_sem,
    recv_sem,
    stat_sem,
):
    req, tp = lax.axis_index("req"), lax.axis_index("tp")
    tp_count = stat_in.shape[0]
    ring = tp_count // 2
    row, x = tp // ring, tp % ring
    tokens, width = residual_ref.shape
    part = tokens // 2

    barrier = pltpu.get_barrier_semaphore()
    for i in range(1, tp_count):
        pl.semaphore_signal(
            barrier, inc=1, device_id=(req, (tp + i) % tp_count), device_id_type=MESH
        )

    right = row * ring + (x + 1) % ring
    left = row * ring + (x + ring - 1) % ring
    other = ((row + 1) % 2) * ring + x

    def send(src, dst, sem, target):
        copy = pltpu.make_async_remote_copy(
            src_ref=src,
            dst_ref=dst,
            send_sem=send_sem.at[sem],
            recv_sem=recv_sem.at[sem],
            device_id=(req, target),
            device_id_type=MESH,
        )
        copy.start()
        return copy

    def block(shift, j):
        owner = ((row + j) % 2) * ring + (x + shift) % ring
        rows = weight_ref[pl.ds(pl.multiple_of(owner * width, width), width), :]
        return lax.dot_general(
            attended_ref[...],
            rows,
            (((1,), (1,)), ((), ())),
            preferred_element_type=jnp.float32,
        ).astype(jnp.bfloat16)

    for j in range(2):
        product = block(2, j)
        for p in range(2):
            far[p, j] = product[p * part : (p + 1) * part]
    pl.semaphore_wait(barrier, tp_count - 1)
    copies = [send(far.at[0], relay_right, 0, right), send(far.at[1], relay_left, 1, left)]
    for j in range(2):
        product = block(1, j)
        for p in range(2):
            to_right[p, j] = product[p * part : (p + 1) * part]
    copies.append(send(to_right.at[1], from_left.at[1], 2, right))
    for j in range(2):
        product = block(ring - 1, j)
        for p in range(2):
            to_left[p, j] = product[p * part : (p + 1) * part]
    copies.append(send(to_left.at[0], from_right.at[0], 3, left))
    for j in range(2):
        product = block(0, j)
        for p in range(2):
            own[p, j] = product[p * part : (p + 1) * part]

    def total(*terms):
        return functools.reduce(jnp.add, [term.astype(jnp.float32) for term in terms])

    copies[0].wait_recv()
    for j in range(2):
        to_right[0, j] = total(to_right[0, j], relay_right[j]).astype(jnp.bfloat16)
    copies.append(send(to_right.at[0], from_left.at[0], 4, right))
    copies[1].wait_recv()
    for j in range(2):
        to_left[1, j] = total(to_left[1, j], relay_left[j]).astype(jnp.bfloat16)
    copies.append(send(to_left.at[1], from_right.at[1], 5, left))
    copies[2].wait_recv()
    copies[3].wait_recv()
    for p in range(2):
        copies[4 + p].wait_recv()
        to_row[p] = total(own[p, 1], from_left[p, 1], from_right[p, 1]).astype(jnp.bfloat16)
        copies.append(send(to_row.at[p], from_row.at[p], 6 + p, other))

    for p in range(2):
        local = total(own[p, 0], from_left[p, 0], from_right[p, 0])
        copies[6 + p].wait_recv()
        span = pl.ds(p * part, part)
        value = residual_ref[span, :].astype(jnp.float32) + gate_ref[...].astype(jnp.float32) * (
            local + from_row[p].astype(jnp.float32)
        )
        updated_ref[span, :] = value
        mean = jnp.sum(value, axis=1, keepdims=True) / width
        variance = jnp.sum(jnp.square(value - mean), axis=1, keepdims=True) / width
        lane = lax.broadcasted_iota(jnp.int32, (part, HD), 1)
        packed = jnp.where(lane == 0, mean, jnp.where(lane == 1, variance, 0.0))
        stat_out[p] = jnp.transpose(packed)[0:8]

    stat_in[tp] = stat_out[...]
    for i in range(1, tp_count):
        copy = pltpu.make_async_remote_copy(
            src_ref=stat_out,
            dst_ref=stat_in.at[tp],
            send_sem=stat_sem.at[0],
            recv_sem=stat_sem.at[1],
            device_id=(req, (tp + i) % tp_count),
            device_id_type=MESH,
        )
        copy.start()
    others = stat_in.at[pl.ds(0, tp_count - 1)]
    pltpu.make_async_copy(others, others, stat_sem.at[1]).wait()
    for p in range(2):
        arrived = [stat_in[i, p] for i in range(tp_count)]
        row_mean = functools.reduce(jnp.add, [a[0:1] for a in arrived]) / tp_count
        row_var = (
            functools.reduce(
                jnp.add, [a[1:2] + jnp.square(a[0:1] - row_mean) for a in arrived]
            )
            / tp_count
        )
        line = lax.broadcasted_iota(jnp.int32, (HD, part), 0)
        stat_ref[pl.ds(p * part, part), :] = jnp.transpose(
            jnp.where(line == 0, row_mean, jnp.where(line == 1, lax.rsqrt(row_var + EPS), 0.0))
        )
    for copy in copies:
        copy.wait_send()
    pltpu.make_async_copy(others, others, stat_sem.at[0]).wait()


def project(attended, weight, residual, gate, tp_count):
    tokens, width = residual.shape
    part = tokens // 2
    vmem = pl.BlockSpec(memory_space=pltpu.VMEM)
    pair = pltpu.VMEM((2, part, width), jnp.bfloat16)
    quad = pltpu.VMEM((2, 2, part, width), jnp.bfloat16)
    stat = pltpu.VMEM((2, 8, part), jnp.float32)
    return pl.pallas_call(
        project_kernel,
        out_shape=(
            jax.ShapeDtypeStruct(residual.shape, jnp.float32),
            jax.ShapeDtypeStruct((tokens, HD), jnp.float32),
        ),
        in_specs=[vmem] * 4,
        out_specs=(vmem, vmem),
        scratch_shapes=[
            quad,
            quad,
            quad,
            pair,
            pair,
            quad,
            quad,
            quad,
            pair,
            pair,
            stat,
            pltpu.VMEM((tp_count, 2, 8, part), jnp.float32),
            pltpu.SemaphoreType.DMA((8,)),
            pltpu.SemaphoreType.DMA((8,)),
            pltpu.SemaphoreType.DMA((2,)),
        ],
        compiler_params=pltpu.CompilerParams(collective_id=1, has_side_effects=True),
    )(attended, weight, residual, gate)


def shards(
    queries,
    new_keys,
    new_values,
    query_gain,
    key_gain,
    cache_keys,
    cache_values,
    page_table,
    cache_lens,
    mig_pages,
    mig_dest,
    cross_queries,
    text_keys,
    text_values,
    out_weight,
    residual,
    gate,
    shift,
    scale,
):
    token_count, local_width = queries.shape
    tp_count = lax.axis_size("tp")
    full_width = local_width * tp_count
    peer_count = lax.axis_size("req")
    page_len = cache_keys.shape[1]
    peers = jnp.arange(peer_count, dtype=jnp.int32)

    destination = mig_dest[:, 0]
    slot_match = (destination[:, None] == peers[None, :]).astype(jnp.int32)
    position = jnp.sum(jnp.cumsum(slot_match, axis=0) * slot_match, axis=1) - 1
    target_slot = destination * CAP + position
    selection = jnp.arange(peer_count * CAP, dtype=jnp.int32)[:, None] == target_slot[None, :]
    slot_page = jnp.sum(jnp.where(selection, mig_pages, 0), axis=1)
    sent_keys = cache_keys[slot_page].reshape(peer_count, CAP * page_len, local_width)
    sent_values = cache_values[slot_page].reshape(peer_count, CAP * page_len, local_width)
    sent_counts = jnp.broadcast_to(
        jnp.sum(slot_match, axis=0)[:, None, None], (peer_count, 1, HD)
    )
    query_float = queries.astype(jnp.float32)
    key_float = new_keys.astype(jnp.float32)
    local_squares = jnp.stack(
        [jnp.sum(query_float * query_float, axis=1), jnp.sum(key_float * key_float, axis=1)]
    )
    arrived_keys, arrived_values, arrivals, all_squares, whole_weight, cross_out = exchange(
        sent_keys,
        sent_values,
        sent_counts,
        local_squares[:, None, :],
        out_weight.T,
        (cross_queries, text_keys, text_values),
        tp_count,
    )
    filled = arrivals[:, 0, :1] > jnp.arange(CAP, dtype=jnp.int32)[None, :]
    arrived_usable = jnp.broadcast_to(
        filled[:, :, None].astype(jnp.float32), (peer_count, CAP, page_len)
    ).reshape(1, -1)
    query_squares, key_squares = jnp.sum(all_squares[:, :, 0, :], axis=0)
    query_normed = (
        query_float * lax.rsqrt(query_squares / full_width + EPS)[:, None] * query_gain
    ).astype(jnp.bfloat16)
    key_normed = (key_float * lax.rsqrt(key_squares / full_width + EPS)[:, None] * key_gain).astype(
        jnp.bfloat16
    )
    own_pages = page_table[0]
    resident_keys = cache_keys[own_pages].reshape(-1, local_width)
    resident_values = cache_values[own_pages].reshape(-1, local_width)
    resident_usable = (
        jnp.arange(resident_keys.shape[0], dtype=jnp.int32) < cache_lens[0]
    ).astype(jnp.float32)[None, :]

    attended = per_head(
        self_kernel,
        (
            query_normed,
            resident_keys,
            resident_values,
            arrived_keys.reshape(-1, local_width),
            arrived_values.reshape(-1, local_width),
            key_normed,
            new_values,
        ),
        (resident_usable, arrived_usable),
        local_width,
    )
    updated, row_stats = project(
        attended,
        whole_weight.reshape(full_width, local_width),
        residual,
        gate,
        tp_count,
    )
    stream = updated.astype(jnp.bfloat16)
    normed = (
        (updated - row_stats[:, :1]) * row_stats[:, 1:2] * (1.0 + scale.astype(jnp.float32))
        + shift.astype(jnp.float32)
    ).astype(jnp.bfloat16)
    return (stream, normed, cross_out)


def solution(mesh):
    in_specs = (
        P("req", "tp"),
        P("req", "tp"),
        P("req", "tp"),
        P("tp"),
        P("tp"),
        P("req", None, "tp"),
        P("req", None, "tp"),
        P("req", None),
        P("req"),
        P("req", None),
        P("req", None),
        P("req", "tp"),
        P("req", "tp"),
        P("req", "tp"),
        P("tp", "req"),
        P("req", "tp"),
        P("req", "tp"),
        P("req", "tp"),
        P("req", "tp"),
    )
    out_specs = (P("req", "tp"), P("req", "tp"), P("req", "tp"))
    return jax.shard_map(shards, mesh=mesh, in_specs=in_specs, out_specs=out_specs, check_vma=False)
```

```python
import functools
import math

import jax
import jax.numpy as jnp
from jax import lax
from jax.experimental import pallas as pl
from jax.experimental.pallas import tpu as pltpu
from jax.sharding import PartitionSpec as P

HD = 128
CAP = 2


EPS = 1e-06


def head_scores(query, keys, scale):
    return (
        lax.dot_general(query, keys, (((1,), (1,)), ((), ())), preferred_element_type=jnp.float32)
        * scale
    )


def self_kernel(q_ref, kr_ref, vr_ref, ka_ref, va_ref, kn_ref, vn_ref, ur_ref, ua_ref, o_ref):
    scale = 1.0 / math.sqrt(HD)
    query = q_ref[...]
    resident = jnp.where(ur_ref[...] > 0, head_scores(query, kr_ref[...], scale), -jnp.inf)
    arrived = jnp.where(ua_ref[...] > 0, head_scores(query, ka_ref[...], scale), -jnp.inf)
    own = head_scores(query, kn_ref[...], scale)
    row_max = jnp.maximum(
        jnp.max(own, axis=1, keepdims=True),
        jnp.maximum(
            jnp.max(resident, axis=1, keepdims=True), jnp.max(arrived, axis=1, keepdims=True)
        ),
    )
    denominator = jnp.zeros_like(row_max)
    mixed = jnp.zeros(o_ref.shape, jnp.float32)
    for scores, values in ((resident, vr_ref), (arrived, va_ref), (own, vn_ref)):
        exponent = jnp.exp(scores - row_max)
        denominator += jnp.sum(exponent, axis=1, keepdims=True)
        mixed += jnp.dot(
            exponent.astype(jnp.bfloat16), values[...], preferred_element_type=jnp.float32
        )
    o_ref[...] = (mixed / denominator).astype(jnp.bfloat16)


def cross_kernel(q_ref, k_ref, v_ref, o_ref):
    scores = head_scores(q_ref[...], k_ref[...], 1.0 / math.sqrt(HD))
    exponent = jnp.exp(scores - jnp.max(scores, axis=1, keepdims=True))
    denominator = jnp.sum(exponent, axis=1, keepdims=True)
    mixed = jnp.dot(exponent.astype(jnp.bfloat16), v_ref[...], preferred_element_type=jnp.float32)
    o_ref[...] = (mixed / denominator).astype(jnp.bfloat16)


def per_head(kernel, rows, masks, width):
    spec = lambda array: pl.BlockSpec((array.shape[0], HD), lambda h: (0, h))
    flag = lambda array: pl.BlockSpec(array.shape, lambda h: (0, 0))
    keys = sum(array.shape[0] for array in rows[1:]) // 2
    tokens = rows[0].shape[0]
    return pl.pallas_call(
        kernel,
        grid=(width // HD,),
        out_shape=jax.ShapeDtypeStruct((tokens, width), jnp.bfloat16),
        in_specs=[spec(array) for array in rows] + [flag(array) for array in masks],
        out_specs=pl.BlockSpec((tokens, HD), lambda h: (0, h)),
        cost_estimate=pl.CostEstimate(
            flops=4 * tokens * keys * width,
            bytes_accessed=4 * (tokens + keys) * width,
            transcendentals=tokens * keys * width // HD,
        ),
    )(*rows, *masks)


MESH = pl.DeviceIdType.MESH


def exchange_kernel(
    layers,
    key_ref,
    value_ref,
    count_ref,
    square_ref,
    weight_ref,
    cross_query_ref,
    text_key_ref,
    text_value_ref,
    key_out,
    value_out,
    count_out,
    square_out,
    weight_out,
    cross_ref,
    page_send,
    page_recv,
    tp_send,
    tp_recv,
    local_sem,
    right_recv,
    left_recv,
    row_recv,
    core_recv,
    weight_send,
):
    peer_count = 4 * layers
    req, tp = lax.axis_index("req"), lax.axis_index("tp")
    tp_count = square_out.shape[0]
    half, layer, core = req // (2 * layers), (req // 2) % layers, req % 2

    def place(h, z, c):
        return (h * layers + z) * 2 + c

    barrier = pltpu.get_barrier_semaphore()

    @pl.loop(1, peer_count)
    def _(i):
        pl.semaphore_signal(
            barrier, inc=1, device_id=((req + i) % peer_count, tp), device_id_type=MESH
        )

    @pl.loop(1, tp_count)
    def _(i):
        pl.semaphore_signal(
            barrier, inc=1, device_id=(req, (tp + i) % tp_count), device_id_type=MESH
        )

    locals_ = [
        pltpu.make_async_copy(key_ref.at[req], key_out.at[req], local_sem.at[0]),
        pltpu.make_async_copy(value_ref.at[req], value_out.at[req], local_sem.at[1]),
        pltpu.make_async_copy(count_ref.at[req], count_out.at[req], local_sem.at[2]),
        pltpu.make_async_copy(square_ref, square_out.at[tp], local_sem.at[3]),
        pltpu.make_async_copy(weight_ref, weight_out.at[req], local_sem.at[4]),
    ]
    for copy in locals_:
        copy.start()
    pl.semaphore_wait(barrier, peer_count + tp_count - 2)

    @pl.loop(1, tp_count)
    def _(i):
        pltpu.make_async_remote_copy(
            src_ref=square_ref,
            dst_ref=square_out.at[tp],
            send_sem=tp_send,
            recv_sem=tp_recv,
            device_id=(req, (tp + i) % tp_count),
            device_id_type=MESH,
        ).start()

    def send_weight(source, origin, target, recv_sem):
        pltpu.make_async_remote_copy(
            src_ref=source,
            dst_ref=weight_out.at[origin],
            send_sem=weight_send,
            recv_sem=recv_sem,
            device_id=(target, tp),
            device_id_type=MESH,
        ).start()

    def wait_block(sem):
        pltpu.make_async_copy(weight_out.at[0], weight_out.at[0], sem).wait()

    right = place(half, (layer + 1) % layers, core)
    left = place(half, (layer + layers - 1) % layers, core)
    across = place((half + 1) % 2, layer, core)
    beside = place(half, layer, (core + 1) % 2)

    def send_pages(target):
        for src, dst, sem in (
            (key_ref, key_out, 0),
            (value_ref, value_out, 1),
            (count_ref, count_out, 2),
        ):
            pltpu.make_async_remote_copy(
                src_ref=src.at[target],
                dst_ref=dst.at[req],
                send_sem=page_send.at[sem],
                recv_sem=page_recv.at[sem],
                device_id=(target, tp),
                device_id_type=MESH,
            ).start()

    def batch(k):
        shift = layers // 2 - (k + 1) // 2
        z = (layer + layers + shift * (2 * (k % 2) - 1)) % layers
        for h in range(2):
            for c in range(2):
                send_pages(place((half + h) % 2, z, (core + c) % 2))

    send_weight(weight_ref, req, right, right_recv.at[0])
    send_weight(weight_ref, req, left, left_recv.at[0])
    send_weight(weight_ref, req, across, row_recv.at[layer])
    send_weight(weight_ref, req, beside, core_recv)
    right_steps = layers // 2
    left_steps = layers - 1 - right_steps
    for h, c in ((0, 1), (1, 0), (1, 1)):
        send_pages(place((half + h) % 2, layer, (core + c) % 2))

    def step(s, from_left, from_right):
        if from_left is not None:
            z = (layer + layers - 1 - s) % layers
            origin = place(half, z, core)
            wait_block(right_recv.at[s])
            if from_left:
                send_weight(weight_out.at[origin], origin, right, right_recv.at[s + 1])
            send_weight(weight_out.at[origin], origin, across, row_recv.at[z])
            send_weight(weight_out.at[origin], origin, beside, core_recv)
        if from_right is not None:
            z = (layer + 1 + s) % layers
            origin = place(half, z, core)
            wait_block(left_recv.at[s])
            if from_right:
                send_weight(weight_out.at[origin], origin, left, left_recv.at[s + 1])
            send_weight(weight_out.at[origin], origin, across, row_recv.at[z])
            send_weight(weight_out.at[origin], origin, beside, core_recv)
        batch(layers - 2 - s)

    @pl.loop(0, left_steps - 1)
    def _(s):
        step(s, True, True)

    for s in range(left_steps - 1, right_steps):
        step(s, s < right_steps - 1, s < left_steps - 1 if s < left_steps else None)

    @pl.loop(0, layers - 1 - right_steps)
    def _(k):
        batch(k)


    @pl.loop(0, layers)
    def _(s):
        z = (layer + layers + ((s + 1) // 2) * (2 * (s % 2) - 1)) % layers
        origin = place((half + 1) % 2, z, core)
        wait_block(row_recv.at[z])
        send_weight(weight_out.at[origin], origin, beside, core_recv)

    for head in range(cross_ref.shape[1] // HD):
        columns = pl.ds(head * HD, HD)
        cross_kernel(
            cross_query_ref.at[:, columns],
            text_key_ref.at[:, columns],
            text_value_ref.at[:, columns],
            cross_ref.at[:, columns],
        )

    for copy in locals_:
        copy.wait()
    halves = weight_out.at[pl.ds(0, 2 * layers)]
    pltpu.make_async_copy(halves, halves, core_recv).wait()
    sent = weight_out.at[pl.ds(0, 4 * layers - 1)]
    pltpu.make_async_copy(sent, sent, weight_send).wait()
    for sem, out in ((0, key_out), (1, value_out), (2, count_out)):
        others = out.at[pl.ds(0, peer_count - 1)]
        pltpu.make_async_copy(others, others, page_recv.at[sem]).wait()
        pltpu.make_async_copy(others, others, page_send.at[sem]).wait()
    others = square_out.at[pl.ds(0, tp_count - 1)]
    pltpu.make_async_copy(others, others, tp_recv).wait()
    pltpu.make_async_copy(others, others, tp_send).wait()


def exchange(keys, values, counts, squares, weight, cross, tp_count):
    peer_count = keys.shape[0]
    layers = peer_count // 4
    anywhere = pl.BlockSpec(memory_space=pl.ANY)
    vmem = pl.BlockSpec(memory_space=pltpu.VMEM)
    shape = jax.ShapeDtypeStruct
    return pl.pallas_call(
        functools.partial(exchange_kernel, layers),
        out_shape=(
            shape(keys.shape, keys.dtype),
            shape(values.shape, values.dtype),
            shape(counts.shape, counts.dtype),
            shape((tp_count,) + squares.shape, squares.dtype),
            shape((peer_count,) + weight.shape, weight.dtype),
            shape(cross[0].shape, cross[0].dtype),
        ),
        in_specs=[anywhere] * 5 + [vmem] * 3,
        out_specs=(anywhere,) * 5 + (vmem,),
        scratch_shapes=[
            pltpu.SemaphoreType.DMA((3,)),
            pltpu.SemaphoreType.DMA((3,)),
            pltpu.SemaphoreType.DMA,
            pltpu.SemaphoreType.DMA,
            pltpu.SemaphoreType.DMA((5,)),
            pltpu.SemaphoreType.DMA((layers,)),
            pltpu.SemaphoreType.DMA((layers,)),
            pltpu.SemaphoreType.DMA((layers,)),
            pltpu.SemaphoreType.DMA,
            pltpu.SemaphoreType.DMA,
        ],
        compiler_params=pltpu.CompilerParams(collective_id=0, has_side_effects=True),
    )(keys, values, counts, squares, weight, *cross)


def project_kernel(
    attended_ref,
    weight_ref,
    residual_ref,
    gate_ref,
    shift_ref,
    scale_ref,
    stream_ref,
    normed_ref,
    far,
    to_right,
    to_left,
    relay_right,
    relay_left,
    from_left,
    from_right,
    own,
    to_row,
    from_row,
    stat_out,
    stat_in,
    send_sem,
    recv_sem,
    stat_sem,
):
    req, tp = lax.axis_index("req"), lax.axis_index("tp")
    tp_count = stat_in.shape[0]
    ring = tp_count // 2
    row, x = tp // ring, tp % ring
    tokens, width = residual_ref.shape
    part = tokens // 2

    barrier = pltpu.get_barrier_semaphore()
    for i in range(1, tp_count):
        pl.semaphore_signal(
            barrier, inc=1, device_id=(req, (tp + i) % tp_count), device_id_type=MESH
        )

    right = row * ring + (x + 1) % ring
    left = row * ring + (x + ring - 1) % ring
    other = ((row + 1) % 2) * ring + x

    def send(src, dst, sem, target):
        copy = pltpu.make_async_remote_copy(
            src_ref=src,
            dst_ref=dst,
            send_sem=send_sem.at[sem],
            recv_sem=recv_sem.at[sem],
            device_id=(req, target),
            device_id_type=MESH,
        )
        copy.start()
        return copy

    def block(shift, j):
        owner = ((row + j) % 2) * ring + (x + shift) % ring
        rows = weight_ref[pl.ds(pl.multiple_of(owner * width, width), width), :]
        return lax.dot_general(
            attended_ref[...],
            rows,
            (((1,), (1,)), ((), ())),
            preferred_element_type=jnp.float32,
        ).astype(jnp.bfloat16)

    for j in range(2):
        product = block(2, j)
        for p in range(2):
            far[p, j] = product[p * part : (p + 1) * part]
    pl.semaphore_wait(barrier, tp_count - 1)
    copies = [send(far.at[0], relay_right, 0, right), send(far.at[1], relay_left, 1, left)]
    for j in range(2):
        product = block(1, j)
        for p in range(2):
            to_right[p, j] = product[p * part : (p + 1) * part]
    copies.append(send(to_right.at[1], from_left.at[1], 2, right))
    for j in range(2):
        product = block(ring - 1, j)
        for p in range(2):
            to_left[p, j] = product[p * part : (p + 1) * part]
    copies.append(send(to_left.at[0], from_right.at[0], 3, left))
    for j in range(2):
        product = block(0, j)
        for p in range(2):
            own[p, j] = product[p * part : (p + 1) * part]

    def total(*terms):
        return functools.reduce(jnp.add, [term.astype(jnp.float32) for term in terms])

    copies[0].wait_recv()
    for j in range(2):
        to_right[0, j] = total(to_right[0, j], relay_right[j]).astype(jnp.bfloat16)
    copies.append(send(to_right.at[0], from_left.at[0], 4, right))
    copies[1].wait_recv()
    for j in range(2):
        to_left[1, j] = total(to_left[1, j], relay_left[j]).astype(jnp.bfloat16)
    copies.append(send(to_left.at[1], from_right.at[1], 5, left))
    copies[2].wait_recv()
    copies[3].wait_recv()
    for p in range(2):
        copies[4 + p].wait_recv()
        to_row[p] = total(own[p, 1], from_left[p, 1], from_right[p, 1]).astype(jnp.bfloat16)
        copies.append(send(to_row.at[p], from_row.at[p], 6 + p, other))

    updated = []
    for p in range(2):
        local = total(own[p, 0], from_left[p, 0], from_right[p, 0])
        copies[6 + p].wait_recv()
        span = pl.ds(p * part, part)
        value = residual_ref[span, :].astype(jnp.float32) + gate_ref[...].astype(jnp.float32) * (
            local + from_row[p].astype(jnp.float32)
        )
        stream_ref[span, :] = value.astype(jnp.bfloat16)
        mean = jnp.sum(value, axis=1, keepdims=True) / width
        variance = jnp.sum(jnp.square(value - mean), axis=1, keepdims=True) / width
        lane = lax.broadcasted_iota(jnp.int32, (part, HD), 1)
        packed = jnp.where(lane == 0, mean, jnp.where(lane == 1, variance, 0.0))
        stat_out[p] = jnp.transpose(packed)[0:8]
        updated.append(value)

    stat_in[tp] = stat_out[...]
    for i in range(1, tp_count):
        copy = pltpu.make_async_remote_copy(
            src_ref=stat_out,
            dst_ref=stat_in.at[tp],
            send_sem=stat_sem.at[0],
            recv_sem=stat_sem.at[1],
            device_id=(req, (tp + i) % tp_count),
            device_id_type=MESH,
        )
        copy.start()
    others = stat_in.at[pl.ds(0, tp_count - 1)]
    pltpu.make_async_copy(others, others, stat_sem.at[1]).wait()
    for p in range(2):
        arrived = [stat_in[i, p] for i in range(tp_count)]
        row_mean = functools.reduce(jnp.add, [a[0:1] for a in arrived]) / tp_count
        row_var = (
            functools.reduce(
                jnp.add, [a[1:2] + jnp.square(a[0:1] - row_mean) for a in arrived]
            )
            / tp_count
        )
        line = lax.broadcasted_iota(jnp.int32, (HD, part), 0)
        packed = jnp.transpose(
            jnp.where(line == 0, row_mean, jnp.where(line == 1, lax.rsqrt(row_var + EPS), 0.0))
        )
        normed = (updated[p] - packed[:, 0:1]) * packed[:, 1:2] * (
            1.0 + scale_ref[...].astype(jnp.float32)
        ) + shift_ref[...].astype(jnp.float32)
        normed_ref[pl.ds(p * part, part), :] = normed.astype(jnp.bfloat16)
    for copy in copies:
        copy.wait_send()
    pltpu.make_async_copy(others, others, stat_sem.at[0]).wait()


def project(attended, weight, residual, gate, shift, scale, tp_count):
    tokens, width = residual.shape
    part = tokens // 2
    vmem = pl.BlockSpec(memory_space=pltpu.VMEM)
    pair = pltpu.VMEM((2, part, width), jnp.bfloat16)
    quad = pltpu.VMEM((2, 2, part, width), jnp.bfloat16)
    stat = pltpu.VMEM((2, 8, part), jnp.float32)
    return pl.pallas_call(
        project_kernel,
        out_shape=(jax.ShapeDtypeStruct(residual.shape, jnp.bfloat16),) * 2,
        in_specs=[vmem] * 6,
        out_specs=(vmem, vmem),
        scratch_shapes=[
            quad,
            quad,
            quad,
            pair,
            pair,
            quad,
            quad,
            quad,
            pair,
            pair,
            stat,
            pltpu.VMEM((tp_count, 2, 8, part), jnp.float32),
            pltpu.SemaphoreType.DMA((8,)),
            pltpu.SemaphoreType.DMA((8,)),
            pltpu.SemaphoreType.DMA((2,)),
        ],
        compiler_params=pltpu.CompilerParams(collective_id=1, has_side_effects=True),
    )(attended, weight, residual, gate, shift, scale)


def shards(
    queries,
    new_keys,
    new_values,
    query_gain,
    key_gain,
    cache_keys,
    cache_values,
    page_table,
    cache_lens,
    mig_pages,
    mig_dest,
    cross_queries,
    text_keys,
    text_values,
    out_weight,
    residual,
    gate,
    shift,
    scale,
):
    token_count, local_width = queries.shape
    tp_count = lax.axis_size("tp")
    full_width = local_width * tp_count
    peer_count = lax.axis_size("req")
    page_len = cache_keys.shape[1]
    peers = jnp.arange(peer_count, dtype=jnp.int32)

    destination = mig_dest[:, 0]
    slot_match = (destination[:, None] == peers[None, :]).astype(jnp.int32)
    position = jnp.sum(jnp.cumsum(slot_match, axis=0) * slot_match, axis=1) - 1
    target_slot = destination * CAP + position
    selection = jnp.arange(peer_count * CAP, dtype=jnp.int32)[:, None] == target_slot[None, :]
    slot_page = jnp.sum(jnp.where(selection, mig_pages, 0), axis=1)
    sent_keys = cache_keys[slot_page].reshape(peer_count, CAP * page_len, local_width)
    sent_values = cache_values[slot_page].reshape(peer_count, CAP * page_len, local_width)
    sent_counts = jnp.broadcast_to(
        jnp.sum(slot_match, axis=0)[:, None, None], (peer_count, 1, HD)
    )
    query_float = queries.astype(jnp.float32)
    key_float = new_keys.astype(jnp.float32)
    local_squares = jnp.stack(
        [jnp.sum(query_float * query_float, axis=1), jnp.sum(key_float * key_float, axis=1)]
    )
    arrived_keys, arrived_values, arrivals, all_squares, whole_weight, cross_out = exchange(
        sent_keys,
        sent_values,
        sent_counts,
        local_squares[:, None, :],
        out_weight.T,
        (cross_queries, text_keys, text_values),
        tp_count,
    )
    filled = arrivals[:, 0, :1] > jnp.arange(CAP, dtype=jnp.int32)[None, :]
    arrived_usable = jnp.broadcast_to(
        filled[:, :, None].astype(jnp.float32), (peer_count, CAP, page_len)
    ).reshape(1, -1)
    query_squares, key_squares = jnp.sum(all_squares[:, :, 0, :], axis=0)
    query_normed = (
        query_float * lax.rsqrt(query_squares / full_width + EPS)[:, None] * query_gain
    ).astype(jnp.bfloat16)
    key_normed = (key_float * lax.rsqrt(key_squares / full_width + EPS)[:, None] * key_gain).astype(
        jnp.bfloat16
    )
    own_pages = page_table[0]
    resident_keys = cache_keys[own_pages].reshape(-1, local_width)
    resident_values = cache_values[own_pages].reshape(-1, local_width)
    resident_usable = (
        jnp.arange(resident_keys.shape[0], dtype=jnp.int32) < cache_lens[0]
    ).astype(jnp.float32)[None, :]

    attended = per_head(
        self_kernel,
        (
            query_normed,
            resident_keys,
            resident_values,
            arrived_keys.reshape(-1, local_width),
            arrived_values.reshape(-1, local_width),
            key_normed,
            new_values,
        ),
        (resident_usable, arrived_usable),
        local_width,
    )
    stream, normed = project(
        attended,
        whole_weight.reshape(full_width, local_width),
        residual,
        gate,
        shift,
        scale,
        tp_count,
    )
    return (stream, normed, cross_out)


def solution(mesh):
    in_specs = (
        P("req", "tp"),
        P("req", "tp"),
        P("req", "tp"),
        P("tp"),
        P("tp"),
        P("req", None, "tp"),
        P("req", None, "tp"),
        P("req", None),
        P("req"),
        P("req", None),
        P("req", None),
        P("req", "tp"),
        P("req", "tp"),
        P("req", "tp"),
        P("tp", "req"),
        P("req", "tp"),
        P("req", "tp"),
        P("req", "tp"),
        P("req", "tp"),
    )
    out_specs = (P("req", "tp"), P("req", "tp"), P("req", "tp"))
    return jax.shard_map(shards, mesh=mesh, in_specs=in_specs, out_specs=out_specs, check_vma=False)
```
